256 devices in a mesh: tr: 32 (over y, z), los: 8 (over x, core).
Axes of the slice: x: 4, y: 4, z: 8, core: 2. Of those that a mesh axis runs over, the one named last changes fastest.
Arguments:
- flux: float32 [64, 65536], P('los', 'tr'), may hold values from -15 to 15
- noise_weight: float32 [64, 65536], P('los', 'tr'), may hold values from 0.2 to 5
- pixel_owner: int32 [65536, 1], P('tr'), may hold values from 0 to 31; in each aligned block of 2048 rows (0 to 2047, 2048 to 4095, ...) at most 128 rows name the same one
- pixel_cell: int32 [65536], P('tr'), may hold values from 0 to 8191
- plane_bin: int32 [64], replicated, may hold values from 0 to 7
- bin_coeffs: float32 [3, 8], replicated, may hold values from 0.25 to 4
Outputs:
- solution: float32 [64, 128, 2048], P('los', 'tr')
- residual: float32 [64, 128, 2048], P('los', 'tr')
The draws below stay inside these ranges and needn't reach their ends.
Inputs may be any that keep to these rules, and one draw needn't show every extreme that they name: `pixel_owner`: among the 2048 pixel rows of one device along tr (aligned blocks) at most 128 name the same strip, a bound that some block reaches of them.
All inputs are finite; a program needn't handle non-finite values.
Results may differ from the reference program's by a relative error of at most 0.00045.
Values sent between devices are 32-bit elements; how exact they have to be, the bound alone decides.
A program may use at most 128 MiB of HBM per device.

```python
import math
import jax
import jax.numpy as jnp
import numpy as np

NZ = 64
SX = 4
GY = 2048
PIX = 2048
NBIN = 8
ITERS = 2
NX = 128
PIX_ALL = 65536
CAP = 128
N_TR = 32


def place_ends(values, key, low, high):
    dims = values.shape
    index_at = [jax.random.randint(jax.random.fold_in(key, axis), (), 0, dims[axis]) for axis in range(len(dims))]
    values = values.at[tuple(index_at)].set(low)
    longest = dims.index(max(dims))
    index_at[longest] = (index_at[longest] + 1) % dims[longest]
    return values.at[tuple(index_at)].set(high)


def steps_of(stream_key, shape, pieces, low, top_value):
    level = 1.0
    for dim, blocks in pieces:
        steps = jax.random.uniform(jax.random.fold_in(jax.random.fold_in(stream_key, 6), dim), (blocks,), jnp.float32, low / len(pieces), top_value / len(pieces))
        level = level * jnp.repeat(jnp.exp(steps), shape[dim] // blocks).reshape((-1,) + (1,) * (len(shape) - 1 - dim))
    return level


def routed_block(own_key, own, number, rows, amount, top, limit, skew):
    ranking = jax.random.permutation(own_key, amount)
    packed, ordinary = shares(amount, rows * top, limit, skew, True), shares(amount, rows * top, limit, skew, False)
    places = jnp.arange(amount)

    def named(tallies, turn):
        used = int((tallies > 0).sum())
        fixed = max(1, used // 4)
        shifted = fixed + (places - fixed + turn * (used - fixed)) % max(1, amount - fixed)
        return jnp.zeros((amount,), jnp.int32).at[ranking[jnp.where(places < fixed, places, shifted)]].set(jnp.asarray(tallies, jnp.int32))

    tallies = jnp.where(number % 4 == 0, named(packed, number // 4), named(ordinary, number - number // 4 - 1))
    mixed = jax.random.permutation(jax.random.fold_in(own, 3), amount)
    source_of, sink = mixed[0:amount // 2 * 2:2], mixed[1:amount // 2 * 2:2]
    room = jnp.minimum(tallies[source_of] - 1, limit - tallies[sink]) // 2
    room = jnp.where((source_of == ranking[0]) | (sink == ranking[0]) | (tallies[sink] == 0), 0, jnp.maximum(room, 0))
    shifted = jax.random.randint(jax.random.fold_in(own, 4), (amount // 2,), 0, 1 << 20) % (room + 1)
    tallies = tallies.at[source_of].add(-shifted).at[sink].add(shifted)
    members = jnp.searchsorted(jnp.cumsum(tallies), jnp.arange(rows * top), side="right").astype(jnp.int32)
    grid = members.reshape(top, rows).T
    grid = grid[jax.random.permutation(jax.random.fold_in(own, 1), rows)]
    turn = jax.random.randint(jax.random.fold_in(own, 2), (rows, 1), 0, top)
    return jnp.take_along_axis(grid, (jnp.arange(top)[None, :] + turn) % top, axis=1)


def shares(amount, total, reach, slope, full):
    loads = [(1 << 20) // math.isqrt(grade ** slope) + 1 for grade in range(1, amount + 1)]
    largest = reach if full else min(reach, max(-(-total // amount), total * loads[0] // sum(loads)))
    least = 1 if total - largest >= amount - 1 else 0
    holding, rest = [largest] + [least] * (amount - 1), total - largest - least * (amount - 1)
    while rest > 0:
        movable = [i for i in range(1, amount) if holding[i] < largest] or [i for i in range(1, amount) if holding[i] < reach]
        whole, budget = sum([loads[i] for i in movable]), rest
        for i in movable:
            addition = min(reach - holding[i], max(1, budget * loads[i] // whole), rest)
            holding[i] = holding[i] + addition
            rest = rest - addition
    return np.array(holding)


def noise(stream_key, extent, width, limit, cuts=(), held_as=jnp.bfloat16):
    array = width * jax.random.normal(stream_key, extent, jnp.float32)
    if cuts:
        array = array * steps_of(stream_key, extent, cuts, -0.22, 0.18)
    return jnp.clip(array, -limit, limit).astype(held_as)


def setup_inputs(seed: int = 0) -> dict:
    key_of = jax.random.split(jax.random.key(seed), 7)
    flux = noise(key_of[0], (NZ, PIX_ALL), 3.0, 15.0, ((0, 8), (1, 32)), jnp.float32)
    noise_weight = jnp.clip(jnp.exp(math.log(5.0) - 3.218876 * jax.random.uniform(key_of[1], (NZ, PIX_ALL), jnp.float32) ** steps_of(key_of[1], (NZ, PIX_ALL), ((0, 8), (1, 32)), -0.2, 0.2)), 0.2, 5.0)
    pixel_owner_keys = jax.random.split(jax.random.fold_in(key_of[2], 1), PIX_ALL // PIX)
    pixel_owner_turns = jax.random.permutation(jax.random.fold_in(key_of[2], 3), PIX_ALL // PIX)
    pixel_owner = jax.vmap(lambda own, number: routed_block(jax.random.fold_in(key_of[2], 2), own, number, PIX, N_TR, 1, CAP, 2))(pixel_owner_keys, pixel_owner_turns).reshape((PIX_ALL, 1))
    pixel_cell = place_ends(jax.random.randint(key_of[3], (PIX_ALL,), 0, SX * GY), jax.random.fold_in(key_of[3], 1), 0, (SX * GY) - 1).astype(jnp.int32)
    plane_bin = place_ends(jax.random.randint(key_of[4], (NZ,), 0, NBIN), jax.random.fold_in(key_of[4], 1), 0, NBIN - 1).astype(jnp.int32)
    bin_coeffs = jnp.clip(jnp.exp(jax.random.uniform(key_of[5], (3, NBIN), jnp.float32, math.log(0.25), math.log(4.0))), 0.25, 4.0)
    return {"flux": flux, "noise_weight": noise_weight, "pixel_owner": pixel_owner, "pixel_cell": pixel_cell, "plane_bin": plane_bin, "bin_coeffs": bin_coeffs}


mass = 0.5


def plane_coeffs(plane_bin, bin_coeffs):
    nbins = bin_coeffs.shape[1]
    match = plane_bin[:, None] == jnp.arange(nbins, dtype=jnp.int32)[None, :]
    rows = [jnp.sum(jnp.where(match, bin_coeffs[k][None, :], jnp.zeros_like(bin_coeffs[k][None, :])), axis=1) for k in range(3)]
    depth = plane_bin.shape[0]
    inside = jnp.arange(depth, dtype=jnp.int32) < depth - 1
    link = jnp.where(inside, rows[2], jnp.zeros_like(rows[2]))
    link_prev = jnp.concatenate([jnp.zeros_like(link[:1]), link[:-1]])
    return rows[0], rows[1], link, link_prev


def smooth_term(field, up_rows, down_rows, diag_field, kx, ky):
    side = jnp.pad(field, ((0, 0), (0, 0), (1, 1)))
    across = kx[:, None, None] * (2.0 * field - up_rows - down_rows)
    along = ky[:, None, None] * (2.0 * field - side[:, :, :-2] - side[:, :, 2:])
    return (diag_field * field + across) + along


def link_term(field, before, after, link, link_prev):
    return link_prev[:, None, None] * (field - before) + link[:, None, None] * (field - after)


def pivot_inverses(diag_field, kx, ky, link, link_prev):
    pivot_d = ((diag_field + 2.0 * kx[:, None, None]) + 2.0 * ky[:, None, None]) + (link_prev + link)[:, None, None]
    inverse = [1.0 / pivot_d[0]]
    for plane in range(1, pivot_d.shape[0]):
        pivot = pivot_d[plane] - (link[plane - 1] * link[plane - 1]) * inverse[plane - 1]
        inverse.append(1.0 / pivot)
    return jnp.stack(inverse)


def column_solve(source, inverse, link):
    depth = source.shape[0]
    forward = [source[0] * inverse[0]]
    for plane in range(1, depth):
        forward.append((source[plane] + link[plane - 1] * forward[plane - 1]) * inverse[plane])
    result = [forward[depth - 1]]
    for plane in range(depth - 2, -1, -1):
        result.append(forward[plane] + (link[plane] * inverse[plane]) * result[-1])
    return jnp.stack(result[::-1])


def apply_operator(field, diag_field, kx, ky, link, link_prev):
    rows_pad = jnp.pad(field, ((0, 0), (1, 1), (0, 0)))
    plane_pad = jnp.pad(field, ((1, 1), (0, 0), (0, 0)))
    smooth = smooth_term(field, rows_pad[:, :-2], rows_pad[:, 2:], diag_field, kx, ky)
    return smooth + link_term(field, plane_pad[:-2], plane_pad[2:], link, link_prev)


def reference(flux, noise_weight, pixel_owner, pixel_cell, plane_bin, bin_coeffs):
    kx, ky, link, link_prev = plane_coeffs(plane_bin, bin_coeffs)
    strip = SX * GY
    target = pixel_owner[:, 0].astype(jnp.int32) * strip + pixel_cell.astype(jnp.int32)
    values = jnp.stack([flux * noise_weight, noise_weight])
    sums = jnp.zeros((2, NZ, NX * GY), jnp.float32).at[:, :, target].add(values)
    sums = sums.reshape(2, NZ, NX, GY)
    right_side = sums[0]
    diag_field = mass + sums[1]
    inverse = pivot_inverses(diag_field, kx, ky, link, link_prev)
    solution = jnp.zeros_like(right_side)
    residual = right_side
    precond = column_solve(residual, inverse, link)
    rz_now = jnp.sum(residual * precond)
    direction = precond
    for step in range(ITERS):
        image = apply_operator(direction, diag_field, kx, ky, link, link_prev)
        alpha = rz_now / jnp.sum(direction * image)
        solution = solution + alpha * direction
        residual = residual - alpha * image
        if step + 1 < ITERS:
            precond = column_solve(residual, inverse, link)
            rz_next = jnp.sum(residual * precond)
            direction = precond + (rz_next / rz_now) * direction
            rz_now = rz_next
    return solution, residual
```

```python
import functools

import jax
import jax.numpy as jnp
from jax import lax
from jax.experimental import pallas as pl
from jax.experimental.pallas import tpu as pltpu
from jax.sharding import PartitionSpec as P

MESH = pl.DeviceIdType.MESH
F32 = jnp.float32
BF16 = jnp.bfloat16
I32 = jnp.int32
SX = 4
CHUNK = 256
CAP = 128
MASS = 0.5
NT = (((1,), (1,)), ((), ()))


def iota(shape, dim):
    return lax.broadcasted_iota(I32, shape, dim)


def two_pieces(values):
    high = values.astype(BF16)
    return high, (values - high.astype(F32)).astype(BF16)


def roll(x, shift, axis):
    size = x.shape[axis]
    return pltpu.roll(x, shift % size if isinstance(shift, int) else shift, axis)


def kernel(
    n_tr, n_los, nzr, flux_ref, weight_ref, owner_ref, cell_ref, bin_ref, coef_ref,
    sol_ref, res_ref,
    xa, xb, pk, rv, acc, sb, tb, kxs, kys, lks, base, inv, gf, zf, qf, wf, sf,
    hs, hr, cs, cr, rb, ps, p1, p2,
    route_send, route_recv, in_send, in_recv, halo_send, halo_recv,
    out_send, out_recv, sum_send, sum_recv, fin_send, fin_recv,
):
    planes, pix = flux_ref.shape
    depth = planes * n_los
    half = depth // 2
    groups = depth // 4
    tr = lax.axis_index("tr")
    los = lax.axis_index("los")
    nyr = n_tr // nzr
    y, zc = tr // nzr, tr % nzr
    offsets = [(dy, dz) for dy in range(nyr) for dz in range(nzr)]
    offsets.sort(key=lambda o: (min(o[0], nyr - o[0]) + min(o[1], nzr - o[1]), o))

    def tr_peer(slot):
        dy, dz = offsets[slot]
        return ((y + dy) % nyr) * nzr + (zc + dz) % nzr

    def los_peer(step):
        return (los + step) % n_los

    def send(src, dst, ssem, rsem, at_tr, at_los):
        return pltpu.make_async_remote_copy(
            src_ref=src, dst_ref=dst, send_sem=ssem, recv_sem=rsem,
            device_id=(at_tr, at_los), device_id_type=MESH,
        )

    @pl.when(tr == 0)
    def _():
        for turn in range(2):
            hr[turn, 0] = jnp.zeros_like(hr[turn, 0])

    @pl.when(tr == n_tr - 1)
    def _():
        for turn in range(2):
            hr[turn, 1] = jnp.zeros_like(hr[turn, 1])

    @pl.when(los == 0)
    def _():
        for turn in range(2):
            cr[turn, 0] = jnp.zeros_like(cr[turn, 0])

    @pl.when(los == n_los - 1)
    def _():
        for turn in range(2):
            cr[turn, 1] = jnp.zeros_like(cr[turn, 1])

    barrier = pltpu.get_barrier_semaphore()
    for slot in range(1, n_tr):
        pl.semaphore_signal(barrier, inc=1, device_id=(tr_peer(slot), los), device_id_type=MESH)
    for step in range(1, n_los):
        pl.semaphore_signal(barrier, inc=1, device_id=(tr, los_peer(step)), device_id_type=MESH)

    owner = owner_ref[...]
    hot = jnp.where(iota((n_tr, pix), 0) == owner, 1.0, 0.0).astype(F32)
    blk = min(256, pix)
    blocks = pix // blk
    stacked = jnp.concatenate(
        [hot[:, b * blk:(b + 1) * blk] for b in range(blocks)], axis=0
    ).astype(BF16)
    before = jnp.where(iota((blk, blk), 0) < iota((blk, blk), 1), 1.0, 0.0).astype(BF16)
    prefix = jnp.dot(stacked, before, preferred_element_type=F32)
    carry = jnp.zeros((n_tr, 1), F32)
    ranks = []
    for b in range(blocks):
        part = hot[:, b * blk:(b + 1) * blk]
        ranks.append(
            jnp.sum(part * (prefix[b * n_tr:(b + 1) * n_tr] + carry), axis=0, keepdims=True)
        )
        carry = carry + jnp.sum(part, axis=1, keepdims=True)
    rank = jnp.concatenate(ranks, axis=1).astype(I32)
    slot_hot = jnp.where(iota((CAP, pix), 0) == rank, 1.0, 0.0).astype(BF16)

    weight = weight_ref[...]
    va, vb = two_pieces(jnp.concatenate([flux_ref[...] * weight, weight], axis=0))
    ca, cb = two_pieces(cell_ref[...].astype(F32))
    chans = 2 * planes
    owner16 = jnp.broadcast_to(owner.astype(F32), (chans, pix)).astype(BF16)
    nothing = jnp.zeros((chans, pix), BF16)
    for o in range(n_tr):
        mine = owner16 == jnp.asarray(o, BF16)
        xa[o * chans:(o + 1) * chans, 0:pix] = jnp.where(mine, va, nothing)
        xb[o * chans:(o + 1) * chans, 0:pix] = jnp.where(mine, vb, nothing)
    top = n_tr * chans
    xa[top:top + n_tr, 0:pix] = (hot * ca.astype(F32)).astype(BF16)
    xb[top:top + n_tr, 0:pix] = (hot * cb.astype(F32)).astype(BF16)
    packed = lax.dot_general(xa[0:top + n_tr, 0:pix], slot_hot, NT, preferred_element_type=F32)
    packed = packed + lax.dot_general(xb[0:top + n_tr, 0:pix], slot_hot, NT, preferred_element_type=F32)
    for o in range(n_tr):
        pk[o, 0:chans, :] = packed[o * chans:(o + 1) * chans, :]
        pk[o, chans:chans + 1, :] = packed[top + o:top + o + 1, :]

    pl.semaphore_wait(barrier, n_tr - 1 + n_los - 1)

    routed = []
    for slot in range(n_tr - 1, 0, -1):
        peer = tr_peer(slot)
        copy = send(pk.at[peer], rv.at[slot], route_send.at[slot], route_recv.at[slot], peer, los)
        copy.start()
        routed.append(copy)
    rv[0] = pk[tr]

    def spread(zi, last):
        b = bin_ref[zi]
        kx = jnp.full((8, 128), coef_ref[0, b], F32)
        ky = jnp.full((8, 128), coef_ref[1, b], F32)
        link = jnp.full((8, 128), coef_ref[2, b], F32)
        link = jnp.where(zi < depth - 1, link, jnp.zeros_like(link))
        kxs[zi] = kx
        kys[zi] = ky
        lks[zi] = link
        base[zi] = MASS + 2.0 * kx + 2.0 * ky + (last + link)
        return link

    lax.fori_loop(0, depth, spread, jnp.zeros((8, 128), F32))

    width = n_los * CHUNK
    jump = min(8, n_tr)
    span = jump * CAP
    by_slot = {n_tr - 1 - i: c for i, c in enumerate(routed)}
    for g in range(n_tr // jump):
        slots = range(g * jump, (g + 1) * jump)
        for slot in slots:
            if slot:
                by_slot[slot].wait_recv()
        vals = jnp.concatenate([rv[slot, 0:chans, :] for slot in slots], axis=1)
        cell = jnp.concatenate([rv[slot, chans:chans + 1, :] for slot in slots], axis=1)
        cell = (cell + 0.5).astype(I32)
        col = cell % width
        place = (col // CHUNK) * SX + cell // width
        low = col % CHUNK
        upper = iota((8, span), 0) < SX
        spreads = [
            jnp.where(
                upper,
                jnp.broadcast_to(vals[p:p + 1], (8, span)),
                jnp.broadcast_to(vals[planes + p:planes + p + 1], (8, span)),
            )
            for p in range(planes)
        ]
        ba, bb = two_pieces(jnp.concatenate(spreads, axis=0))
        low_hot = jnp.where(iota((CHUNK, span), 0) == low, 1.0, 0.0).astype(BF16)
        where_to = (
            jnp.broadcast_to(place, (16, span)) - iota((16, span), 0) % SX
        ).astype(F32).astype(BF16)
        none = jnp.zeros((16, span), BF16)
        rows = 8 * planes
        for k in range(n_los):
            mine = where_to == jnp.asarray(SX * k, BF16)
            for t in range(rows // 16):
                at = k * rows + 16 * t
                xa[at:at + 16, 0:span] = jnp.where(mine, ba[16 * t:16 * t + 16], none)
                xb[at:at + 16, 0:span] = jnp.where(mine, bb[16 * t:16 * t + 16], none)
        full = n_los * rows
        part = lax.dot_general(xa[0:full, 0:span], low_hot, NT, preferred_element_type=F32)
        part = part + lax.dot_general(xb[0:full, 0:span], low_hot, NT, preferred_element_type=F32)
        if g == 0:
            acc[...] = part
        else:
            acc[...] = acc[...] + part

    upper3 = iota((planes, 8, 128), 1) < SX
    for k in range(n_los):
        both = acc[k * 8 * planes:(k + 1) * 8 * planes, :]
        left = both[:, 0:128].reshape(planes, 8, 128)
        right = both[:, 128:256].reshape(planes, 8, 128)
        sb[k * planes:(k + 1) * planes, 0] = jnp.where(upper3, left, roll(right, 4, 1))
        sb[k * planes:(k + 1) * planes, 1] = jnp.where(upper3, roll(left, 4, 1), right)
    here = pl.ds(los * planes, planes)
    entered = []
    for step in range(1, n_los):
        peer = los_peer(step)
        copy = send(
            sb.at[pl.ds(peer * planes, planes)], tb.at[here],
            in_send.at[step], in_recv.at[step], tr, peer,
        )
        copy.start()
        entered.append(copy)
    tb[here] = sb[here]
    for copy in entered:
        copy.wait_recv()

    stride = min(8, half)
    zero = jnp.zeros((8, 128), F32)

    def pivots(block, state):
        it, gt, lt, ib, gb = state
        for u in range(stride):
            zt = block * stride + u
            zb = depth - 1 - zt
            it = 1.0 / ((base[zt] + tb[zt, 1]) - (lt * lt) * it)
            gt = (tb[zt, 0] + lt * gt) * it
            lb = lks[zb]
            ib = 1.0 / ((base[zb] + tb[zb, 1]) - (lb * lb) * ib)
            gb = (tb[zb, 0] + lb * gb) * ib
            lt = lks[zt]
            inv[zt] = it
            gf[zt] = gt
            inv[zb] = ib
            gf[zb] = gb
        return it, gt, lt, ib, gb

    it, gt, lt, ib, gb = lax.fori_loop(0, half // stride, pivots, (zero,) * 5)
    ratio_top, ratio_bottom = lt * it, lt * ib
    middle = 1.0 / (1.0 - ratio_top * ratio_bottom)

    def eliminate(block, state):
        gt, lt, gb = state
        for u in range(stride):
            zt = block * stride + u
            zb = depth - 1 - zt
            gt = (qf[zt] + lt * gt) * inv[zt]
            gb = (qf[zb] + lks[zb] * gb) * inv[zb]
            lt = lks[zt]
            gf[zt] = gt
            gf[zb] = gb
        return gt, lt, gb

    def back(out, source, gt, gb):
        yt = (gt + ratio_top * gb) * middle
        yb = gb + ratio_bottom * yt
        out[half - 1] = yt
        out[half] = yb
        total = source(half - 1) * yt + source(half) * yb

        def one(zt, state):
            yt, yb, total = state
            zb = depth - 1 - zt
            yt = gf[zt] + (lks[zt] * inv[zt]) * yt
            yb = gf[zb] + (lks[zb - 1] * inv[zb]) * yb
            out[zt] = yt
            out[zb] = yb
            return yt, yb, total + (source(zt) * yt + source(zb) * yb)

        state = (yt, yb, total)
        for u in range(stride - 1):
            state = one(half - 2 - u, state)

        def some(block, state):
            for u in range(stride):
                state = one(half - 1 - (block * stride + u), state)
            return state

        return lax.fori_loop(1, half // stride, some, state)[2]

    sub = iota((8, 128), 0)
    lane = iota((8, 128), 1)
    quarter = sub % 4
    first_row, last_row = quarter == 0, quarter == 3
    at_left, at_right = lane == 0, lane == 127
    inner_left, inner_right = at_left & (sub >= 4), at_right & (sub < 4)

    def edges(field, turn):
        def rows(i, state):
            left, right = state
            down = up = zero
            for j in range(4):
                zi = i * 4 + j
                v = field[zi]
                down = jnp.where(quarter == j, roll(v, j - 3, 0), down)
                up = jnp.where(quarter == j, roll(v, j, 0), up)
                u = roll(v, 4, 0)
                here_lane = lane == zi
                right = jnp.where(here_lane, roll(u, zi + 1, 1), right)
                left = jnp.where(here_lane, roll(u, zi, 1), left)
            hs[turn, 0, i] = down
            hs[turn, 1, i] = up
            return left, right

        left, right = lax.fori_loop(0, groups, rows, (zero, zero))
        cs[turn, 0] = right
        cs[turn, 1] = left

        def moves(side):
            step = 1 if side == 0 else -1
            last_tr, last_los = (n_tr - 1, n_los - 1) if side == 0 else (0, 0)
            row = send(
                hs.at[turn, side], hr.at[turn, side], halo_send.at[turn, side, 0],
                halo_recv.at[turn, side, 0], (tr + step + n_tr) % n_tr, los,
            )
            column = send(
                cs.at[turn, side], cr.at[turn, side], halo_send.at[turn, side, 1],
                halo_recv.at[turn, side, 1], tr, (los + step + n_los) % n_los,
            )
            return row, column, tr != last_tr, los != last_los

        for side in range(2):
            row, column, has_row, has_column = moves(side)
            pl.when(has_row)(row.start)
            pl.when(has_column)(column.start)
        return [moves(side) for side in range(2)]

    def edges_arrive(moved):
        for side in range(2):
            row, column, has_row, has_column = moved[side]
            pl.when(has_row)(row.wait_send)
            pl.when(has_column)(column.wait_send)
        for side in range(2):
            row, column, _, _ = moved[side]
            first_tr, first_los = (0, 0) if side == 0 else (n_tr - 1, n_los - 1)
            pl.when(tr != first_tr)(row.wait_recv)
            pl.when(los != first_los)(column.wait_recv)

    def operate(field, turn, source, out):
        from_left, from_right = cr[turn, 0], cr[turn, 1]

        def some(i, total):
            above, below = hr[turn, 0, i], hr[turn, 1, i]
            for j in range(4):
                zi = i * 4 + j
                v = field[zi]
                up = jnp.where(first_row, roll(above, -j, 0), roll(v, 1, 0))
                down = jnp.where(last_row, roll(below, 3 - j, 0), roll(v, -1, 0))
                u = roll(v, 4, 0)
                before = jnp.where(at_left, roll(from_left, 128 - zi, 1), roll(v, 1, 1))
                before = jnp.where(inner_left, roll(u, 1, 1), before)
                after = jnp.where(at_right, roll(from_right, 127 - zi, 1), roll(v, 127, 1))
                after = jnp.where(inner_right, roll(u, 127, 1), after)
                image = source(zi) - (kxs[zi] * (up + down) + kys[zi] * (before + after))
                out[zi] = image
                total = total + v * image
            return total

        return lax.fori_loop(0, groups, some, zero)

    def leave(field, which):
        copies = []
        for step in range(1, n_los):
            peer = los_peer(step)
            copy = send(
                field.at[pl.ds(peer * planes, planes)], rb.at[which, los],
                out_send.at[which, step], out_recv.at[which, step], tr, peer,
            )
            copy.start()
            copies.append(copy)
        rb[which, los] = field[here]
        return copies

    right_side = lambda zi: tb[zi, 0]
    image_of = lambda zi: qf[zi]
    dot_bz = back(zf, right_side, gt, gb)
    moved = edges(zf, 0)
    left_z = leave(zf, 0)
    edges_arrive(moved)
    dot_zq = operate(zf, 0, right_side, qf)

    gt, _, gb = lax.fori_loop(0, half // stride, eliminate, (zero,) * 3)
    dot_qw = back(wf, image_of, gt, gb)
    moved = edges(wf, 1)
    left_q = leave(qf, 1)
    left_w = leave(wf, 2)
    edges_arrive(moved)
    dot_ws = operate(wf, 1, image_of, sf)

    for n, dot in enumerate((dot_bz, dot_zq, dot_qw, dot_ws)):
        ps[0, n:n + 1, :] = jnp.sum(dot, axis=0, keepdims=True)
    summed = []
    for slot in range(n_tr - 1, 0, -1):
        copy = send(
            ps.at[0], p1.at[slot], sum_send.at[slot], sum_recv.at[slot], tr_peer(slot), los
        )
        copy.start()
        summed.append(copy)
    left_s = leave(sf, 3)
    total = ps[0]
    for copy in summed:
        copy.wait_recv()
    for slot in range(1, n_tr):
        total = total + p1[slot]
    ps[1] = total
    finals = []
    for step in range(1, n_los):
        copy = send(
            ps.at[1], p2.at[step], fin_send.at[step], fin_recv.at[step], tr, los_peer(step)
        )
        copy.start()
        finals.append(copy)
    for copy in finals:
        copy.wait_recv()
    for step in range(1, n_los):
        total = total + p2[step]
    total = jnp.sum(total, axis=1, keepdims=True)
    bz, zq, qw, ws = (
        jnp.broadcast_to(total[n:n + 1], (8, 128)) for n in range(4)
    )
    alpha = bz / zq
    rz = alpha * alpha * qw - bz
    beta = rz / bz
    grown = 1.0 + beta
    alpha_next = rz / (grown * grown * zq - 2.0 * grown * alpha * qw + alpha * alpha * ws)
    main = alpha + alpha_next * grown
    other = alpha * alpha_next

    for copies in (left_z, left_w, left_q, left_s):
        for copy in copies:
            copy.wait_recv()

    def finish(k, none):
        for p in range(planes):
            x = main * rb[0, k, p] - other * rb[2, k, p]
            r = sb[k * planes + p, 0] - main * rb[1, k, p] + other * rb[3, k, p]
            for part in range(2):
                at = pl.ds(pl.multiple_of(k * CHUNK + part * 128, 128), 128)
                sol_ref[p, :, at] = x[part * SX:(part + 1) * SX]
                res_ref[p, :, at] = r[part * SX:(part + 1) * SX]
        return none

    lax.fori_loop(0, n_los, finish, 0)

    for copies in (routed, entered, left_z, left_q, left_w, left_s, summed, finals):
        for copy in copies:
            copy.wait_send()


def local(flux, noise_weight, pixel_owner, pixel_cell, plane_bin, bin_coeffs):
    n_tr, n_los = lax.axis_size("tr"), lax.axis_size("los")
    nzr = 8 if n_tr == 32 else 2
    planes, pix = flux.shape
    depth = planes * n_los
    cols = n_los * CHUNK
    dma = pltpu.SemaphoreType.DMA
    full = pltpu.VMEM((depth, 8, 128), F32)
    vmem = pl.BlockSpec(memory_space=pltpu.VMEM)
    smem = pl.BlockSpec(memory_space=pltpu.SMEM)
    top = (n_tr * 2 * planes) + n_tr
    out = jax.ShapeDtypeStruct((planes, SX, cols), F32)
    return pl.pallas_call(
        functools.partial(kernel, n_tr, n_los, nzr),
        out_shape=(out, out),
        in_specs=[vmem, vmem, vmem, vmem, smem, smem],
        out_specs=(vmem, vmem),
        scratch_shapes=[
            pltpu.VMEM((max(top, n_los * 8 * planes), max(pix, min(8, n_tr) * CAP)), BF16),
            pltpu.VMEM((max(top, n_los * 8 * planes), max(pix, min(8, n_tr) * CAP)), BF16),
            pltpu.VMEM((n_tr, 2 * planes + 1, CAP), F32),
            pltpu.VMEM((n_tr, 2 * planes + 1, CAP), F32),
            pltpu.VMEM((n_los * 8 * planes, CHUNK), F32),
            pltpu.VMEM((depth, 2, 8, 128), F32),
            pltpu.VMEM((depth, 2, 8, 128), F32),
            full, full, full, full, full, full, full, full, full, full,
            pltpu.VMEM((2, 2, depth // 4, 8, 128), F32),
            pltpu.VMEM((2, 2, depth // 4, 8, 128), F32),
            pltpu.VMEM((2, 2, 8, 128), F32),
            pltpu.VMEM((2, 2, 8, 128), F32),
            pltpu.VMEM((4, n_los, planes, 8, 128), F32),
            pltpu.VMEM((2, 4, 128), F32),
            pltpu.VMEM((n_tr, 4, 128), F32),
            pltpu.VMEM((n_los, 4, 128), F32),
            dma((n_tr,)), dma((n_tr,)), dma((n_los,)), dma((n_los,)),
            dma((2, 2, 2)), dma((2, 2, 2)), dma((4, n_los)), dma((4, n_los)),
            dma((n_tr,)), dma((n_tr,)), dma((n_los,)), dma((n_los,)),
        ],
        compiler_params=pltpu.CompilerParams(
            collective_id=0, has_side_effects=True, vmem_limit_bytes=50 * 1024 * 1024
        ),
        name="wiener",
    )(
        flux, noise_weight, pixel_owner.reshape(1, pix), pixel_cell.reshape(1, pix),
        plane_bin, bin_coeffs,
    )


def solution(mesh):
    placed = (P("los", "tr"), P("los", "tr"), P("tr", None), P("tr"), P(), P())
    return jax.shard_map(
        local,
        mesh=mesh,
        in_specs=placed,
        out_specs=(P("los", "tr", None), P("los", "tr", None)),
        check_vma=False,
    )
```

```python
import functools

import jax
import jax.numpy as jnp
from jax import lax
from jax.experimental import pallas as pl
from jax.experimental.pallas import tpu as pltpu
from jax.sharding import PartitionSpec as P

MESH = pl.DeviceIdType.MESH
F32 = jnp.float32
BF16 = jnp.bfloat16
I32 = jnp.int32
SX = 4
CHUNK = 256
CAP = 128
MASS = 0.5
NT = (((1,), (1,)), ((), ()))


def iota(shape, dim):
    return lax.broadcasted_iota(I32, shape, dim)


def two_pieces(values):
    high = values.astype(BF16)
    return high, (values - high.astype(F32)).astype(BF16)


def roll(x, shift, axis):
    size = x.shape[axis]
    return pltpu.roll(x, shift % size if isinstance(shift, int) else shift, axis)


def kernel(
    n_tr, n_los, nzr, flux_hbm, weight_hbm, owner_hbm, cell_hbm, bin_hbm, coef_hbm,
    sol_ref, res_ref,
    flux_ref, weight_ref, owner_ref, cell_ref, bin_ref, coef_ref,
    xp, xs, pw, pf, rw, rf, lows, dests, acc, sw, sf, tw, tf,
    kxs, kys, lks, base, inv, gf, zf, qf, wf, vf, pre,
    hs, hr, cs, cr, rb, ps, p1, p2,
    load_sem, route_send, route_recv, in_send, in_recv, halo_send, halo_recv,
    out_send, out_recv, sum_send, sum_recv, fin_send, fin_recv,
):
    planes, pix = flux_ref.shape
    depth = planes * n_los
    half = depth // 2
    groups = depth // 4
    tr = lax.axis_index("tr")
    los = lax.axis_index("los")
    nyr = n_tr // nzr
    y, zc = tr // nzr, tr % nzr
    offsets = [(dy, dz) for dy in range(nyr) for dz in range(nzr)]
    offsets.sort(key=lambda o: (min(o[0], nyr - o[0]) + min(o[1], nzr - o[1]), o))
    far_steps = sorted(range(1, n_los), key=lambda d: -min(d, n_los - d))

    def tr_peer(slot):
        dy, dz = offsets[slot]
        return ((y + dy) % nyr) * nzr + (zc + dz) % nzr

    def los_peer(step):
        return (los + step) % n_los

    def send(src, dst, ssem, rsem, at_tr, at_los):
        return pltpu.make_async_remote_copy(
            src_ref=src, dst_ref=dst, send_sem=ssem, recv_sem=rsem,
            device_id=(at_tr, at_los), device_id_type=MESH,
        )

    loads = [
        pltpu.make_async_copy(src, dst, load_sem.at[n])
        for n, (src, dst) in enumerate((
            (owner_hbm, owner_ref), (weight_hbm, weight_ref), (cell_hbm, cell_ref),
            (flux_hbm, flux_ref), (bin_hbm, bin_ref), (coef_hbm, coef_ref),
        ))
    ]
    for load in loads:
        load.start()

    @pl.when(tr == 0)
    def _():
        for turn in range(2):
            hr[turn, 0] = jnp.zeros_like(hr[turn, 0])

    @pl.when(tr == n_tr - 1)
    def _():
        for turn in range(2):
            hr[turn, 1] = jnp.zeros_like(hr[turn, 1])

    @pl.when(los == 0)
    def _():
        for turn in range(2):
            cr[turn, 0] = jnp.zeros_like(cr[turn, 0])

    @pl.when(los == n_los - 1)
    def _():
        for turn in range(2):
            cr[turn, 1] = jnp.zeros_like(cr[turn, 1])

    barrier = pltpu.get_barrier_semaphore()
    for slot in range(n_tr - 1, 0, -1):
        pl.semaphore_signal(barrier, inc=1, device_id=(tr_peer(slot), los), device_id_type=MESH)
    for step in far_steps:
        pl.semaphore_signal(barrier, inc=1, device_id=(tr, los_peer(step)), device_id_type=MESH)

    loads[0].wait()
    owner = owner_ref[...]
    hot = jnp.where(iota((n_tr, pix), 0) == owner, 1.0, 0.0).astype(F32)
    blk = min(256, pix)
    blocks = pix // blk
    stacked = jnp.concatenate(
        [hot[:, b * blk:(b + 1) * blk] for b in range(blocks)], axis=0
    ).astype(BF16)
    before = jnp.where(iota((blk, blk), 0) < iota((blk, blk), 1), 1.0, 0.0).astype(BF16)
    prefix = jnp.dot(stacked, before, preferred_element_type=F32)
    carry = jnp.zeros((n_tr, 1), F32)
    ranks = []
    for b in range(blocks):
        part = hot[:, b * blk:(b + 1) * blk]
        ranks.append(
            jnp.sum(part * (prefix[b * n_tr:(b + 1) * n_tr] + carry), axis=0, keepdims=True)
        )
        carry = carry + jnp.sum(part, axis=1, keepdims=True)
    rank = jnp.concatenate(ranks, axis=1).astype(I32)
    slot_hot = jnp.where(iota((CAP, pix), 0) == rank, 1.0, 0.0).astype(BF16)
    pair = 16 // planes
    owner16 = (
        jnp.broadcast_to(owner, (16, pix)) - iota((16, pix), 0) // planes
    ).astype(F32).astype(BF16)
    nothing = jnp.zeros((16, pix), BF16)
    rows = n_tr * planes

    def spread_by_owner(values, at):
        twice = jnp.concatenate([values] * pair, axis=0)
        for o in range(0, n_tr, pair):
            xp[at + o * planes:at + (o + pair) * planes, :] = jnp.where(
                owner16 == jnp.asarray(o, BF16), twice, nothing
            )

    for load in loads[1:]:
        load.wait()
    weight = weight_ref[...]
    wa, wb = two_pieces(weight)
    ca, cb = two_pieces(cell_ref[...].astype(F32))
    extra = rows + n_tr
    spread_by_owner(wa, 0)
    spread_by_owner(wb, extra)
    xp[rows:extra, :] = (hot * ca.astype(F32)).astype(BF16)
    xp[extra + rows:2 * extra, :] = (hot * cb.astype(F32)).astype(BF16)
    packed = lax.dot_general(xp[...], slot_hot, NT, preferred_element_type=F32)
    packed = packed[0:extra] + packed[extra:2 * extra]
    for o in range(n_tr):
        pw[o, 0:planes, :] = packed[o * planes:(o + 1) * planes]
        pw[o, planes:planes + 1, :] = packed[rows + o:rows + o + 1]

    pl.semaphore_wait(barrier, n_tr - 1 + n_los - 1)

    routed = [None], [None]

    def route(stage, packs, into):
        for slot in range(1, n_tr):
            peer = tr_peer(slot)
            routed[stage].append(send(
                packs.at[peer], into.at[slot],
                route_send.at[stage, slot], route_recv.at[stage, slot], peer, los,
            ))
        for copy in routed[stage][:0:-1]:
            copy.start()

    route(0, pw, rw)
    rw[0] = pw[tr]

    fa, fb = two_pieces(flux_ref[...] * weight)
    spread_by_owner(fa, 0)
    spread_by_owner(fb, rows)
    packed = lax.dot_general(xp[0:2 * rows, :], slot_hot, NT, preferred_element_type=F32)
    packed = packed[0:rows] + packed[rows:2 * rows]
    for o in range(n_tr):
        pf[o] = packed[o * planes:(o + 1) * planes]
    route(1, pf, rf)
    rf[0] = pf[tr]

    def spread(zi, last):
        b = bin_ref[zi]
        kx = jnp.full((8, 128), coef_ref[0, b], F32)
        ky = jnp.full((8, 128), coef_ref[1, b], F32)
        link = jnp.full((8, 128), coef_ref[2, b], F32)
        link = jnp.where(zi < depth - 1, link, jnp.zeros_like(link))
        kxs[zi] = kx
        kys[zi] = ky
        lks[zi] = link
        base[zi] = MASS + 2.0 * kx + 2.0 * ky + (last + link)
        return link

    lax.fori_loop(0, depth, spread, jnp.zeros((8, 128), F32))

    width = n_los * CHUNK
    jump = min(8, n_tr)
    span = jump * CAP
    chunks = n_tr // jump
    each = SX * planes
    full = n_los * each
    upper = iota((8, span), 0) < SX
    low_iota = iota((CHUNK, span), 0)
    row16 = iota((16, span), 0) % SX
    none = jnp.zeros((16, span), BF16)
    upper3 = iota((planes // 2, 8, 128), 1) < SX

    def scatter(stage, arrived):
        for g in range(chunks - 1, -1, -1):
            slots = range(g * jump, (g + 1) * jump)
            for slot in reversed(slots):
                if slot:
                    routed[stage][slot].wait_recv()
            if stage == 0:
                cell = jnp.concatenate([arrived[t, planes:planes + 1, :] for t in slots], axis=1)
                cell = (cell + 0.5).astype(I32)
                col = cell % width
                place = (col // CHUNK) * SX + cell // width
                low = jnp.broadcast_to(col % CHUNK, (CHUNK, span))
                lows[g] = jnp.where(low_iota == low, 1.0, 0.0).astype(BF16)
                dests[g] = (
                    jnp.broadcast_to(place, (16, span)) - row16
                ).astype(F32).astype(BF16)
            vals = jnp.concatenate([arrived[t, 0:planes, :] for t in slots], axis=1)
            ba, bb = two_pieces(jnp.concatenate([
                jnp.where(
                    upper,
                    jnp.broadcast_to(vals[p:p + 1], (8, span)),
                    jnp.broadcast_to(vals[p + 1:p + 2], (8, span)),
                )
                for p in range(0, planes, 2)
            ], axis=0))
            dest = dests[g]
            for k in range(n_los):
                mine = dest == jnp.asarray(SX * k, BF16)
                for t in range(0, each, 16):
                    at = k * each + t
                    xs[at:at + 16, :] = jnp.where(mine, ba[t:t + 16], none)
                    xs[full + at:full + at + 16, :] = jnp.where(mine, bb[t:t + 16], none)
            part = lax.dot_general(xs[...], lows[g], NT, preferred_element_type=F32)
            part = part[0:full] + part[full:2 * full]
            if g == chunks - 1:
                acc[...] = part
            else:
                acc[...] = acc[...] + part

    here = pl.ds(los * planes, planes)

    def enter(stage, out, into):
        for k in range(n_los):
            both = acc[k * each:(k + 1) * each, :]
            left = both[:, 0:128].reshape(planes // 2, 8, 128)
            right = both[:, 128:256].reshape(planes // 2, 8, 128)
            even = jnp.where(upper3, left, roll(right, 4, 1))
            odd = jnp.where(upper3, roll(left, 4, 1), right)
            for p in range(planes // 2):
                out[k * planes + 2 * p] = even[p]
                out[k * planes + 2 * p + 1] = odd[p]
        copies = []
        for step in far_steps:
            peer = los_peer(step)
            copy = send(
                out.at[pl.ds(peer * planes, planes)], into.at[here],
                in_send.at[stage, step], in_recv.at[stage, step], tr, peer,
            )
            copy.start()
            copies.append(copy)
        into[here] = out[here]
        return copies

    scatter(0, rw)
    entered_w = enter(0, sw, tw)
    scatter(1, rf)
    entered_f = enter(1, sf, tf)

    for copy in entered_w:
        copy.wait_recv()

    stride = min(8, half)
    zero = jnp.zeros((8, 128), F32)

    def pivots(block, state):
        it, lt, ib = state
        for u in range(stride):
            zt = block * stride + u
            zb = depth - 1 - zt
            it = 1.0 / ((base[zt] + tw[zt]) - (lt * lt) * it)
            lb = lks[zb]
            ib = 1.0 / ((base[zb] + tw[zb]) - (lb * lb) * ib)
            lt = lks[zt]
            inv[zt] = it
            inv[zb] = ib
        return it, lt, ib

    it, lt, ib = lax.fori_loop(0, half // stride, pivots, (zero,) * 3)
    ratio_top, ratio_bottom = lt * it, lt * ib
    middle = 1.0 / (1.0 - ratio_top * ratio_bottom)

    def solve(source, out):
        def eliminate(block, state):
            gt, lt, gb = state
            for u in range(stride):
                zt = block * stride + u
                zb = depth - 1 - zt
                gt = (source[zt] + lt * gt) * inv[zt]
                gb = (source[zb] + lks[zb] * gb) * inv[zb]
                lt = lks[zt]
                gf[zt] = gt
                gf[zb] = gb
            return gt, lt, gb

        gt, _, gb = lax.fori_loop(0, half // stride, eliminate, (zero,) * 3)
        yt = (gt + ratio_top * gb) * middle
        yb = gb + ratio_bottom * yt
        out[half - 1] = yt
        out[half] = yb
        total = source[half - 1] * yt + source[half] * yb

        def one(zt, state):
            yt, yb, total = state
            zb = depth - 1 - zt
            yt = gf[zt] + (lks[zt] * inv[zt]) * yt
            yb = gf[zb] + (lks[zb - 1] * inv[zb]) * yb
            out[zt] = yt
            out[zb] = yb
            return yt, yb, total + (source[zt] * yt + source[zb] * yb)

        state = (yt, yb, total)
        for u in range(stride - 1):
            state = one(half - 2 - u, state)

        def some(block, state):
            for u in range(stride):
                state = one(half - 1 - (block * stride + u), state)
            return state

        return lax.fori_loop(1, half // stride, some, state)[2]

    sub = iota((8, 128), 0)
    lane = iota((8, 128), 1)
    quarter = sub % 4
    first_row, last_row = quarter == 0, quarter == 3
    in_half = sub < 4
    inner_left, inner_right = (lane == 0) & ~in_half, (lane == 127) & in_half
    outer = ((lane == 0) & in_half) | ((lane == 127) & ~in_half)

    def edge_copy(turn, side, kind):
        step = 1 if side == 0 else -1
        if kind == 0:
            src, dst, where = hs.at[turn, side], hr.at[turn, side], (
                (tr + step + n_tr) % n_tr, los)
        else:
            src, dst, where = cs.at[turn], cr.at[turn, side], (tr, (los + step + n_los) % n_los)
        return send(
            src, dst, halo_send.at[turn, side, kind], halo_recv.at[turn, side, kind], *where
        )

    def edge_each(turn, kind, what):
        for side in range(2):
            copy = edge_copy(turn, side, kind)
            here_is, size = (tr, n_tr) if kind == 0 else (los, n_los)
            first, last = (0, size - 1) if side == 0 else (size - 1, 0)
            if what == "start":
                pl.when(here_is != last)(copy.start)
            elif what == "sent":
                pl.when(here_is != last)(copy.wait_send)
            else:
                pl.when(here_is != first)(copy.wait_recv)

    wide = 8

    def edge_rows(field, turn):
        def pack(block, none):
            for i in range(2):
                down = up = zero
                for j in range(4):
                    v = field[block * wide + i * 4 + j]
                    down = jnp.where(quarter == j, roll(v, j - 3, 0), down)
                    up = jnp.where(quarter == j, roll(v, j, 0), up)
                hs[turn, 0, block * 2 + i] = down
                hs[turn, 1, block * 2 + i] = up
            return none

        lax.fori_loop(0, depth // wide, pack, 0)
        edge_each(turn, 0, "start")

    def edge_columns(field, turn):
        def pack(block, found):
            for i in range(wide):
                zi = block * wide + i
                u = roll(field[zi], 4, 0)
                both = jnp.where(in_half, roll(u, 1, 1), u)
                found = jnp.where(lane == zi, roll(both, zi, 1), found)
            return found

        cs[turn] = lax.fori_loop(0, depth // wide, pack, zero)
        edge_each(turn, 1, "start")

    def operate_inside(field, source):
        def some(block, none):
            for i in range(wide):
                zi = block * wide + i
                v = field[zi]
                u = roll(v, 4, 0)
                up = jnp.where(first_row, 0.0, roll(v, 1, 0))
                down = jnp.where(last_row, 0.0, roll(v, -1, 0))
                before = jnp.where(inner_left, roll(u, 1, 1), roll(v, 1, 1))
                after = jnp.where(inner_right, roll(u, 127, 1), roll(v, 127, 1))
                beside = jnp.where(in_half & (lane == 0), after, before + after)
                beside = jnp.where((lane == 127) & ~in_half, before, beside)
                pre[zi] = source[zi] - (kxs[zi] * (up + down) + kys[zi] * beside)
            return none

        lax.fori_loop(0, depth // wide, some, 0)

    def operate_edges(field, turn, out):
        columns = jnp.where(in_half, cr[turn, 0], roll(cr[turn, 1], 127, 1))

        def some(block, total):
            for i in range(wide):
                zi = block * wide + i
                j = i % 4
                above, below = hr[turn, 0, block * 2 + i // 4], hr[turn, 1, block * 2 + i // 4]
                rows = jnp.where(
                    first_row, roll(above, -j, 0), jnp.where(last_row, roll(below, 3 - j, 0), 0.0)
                )
                beside = jnp.where(outer, roll(columns, 128 - zi, 1), 0.0)
                image = pre[zi] - (kxs[zi] * rows + kys[zi] * beside)
                out[zi] = image
                total = total + field[zi] * image
            return total

        return lax.fori_loop(0, depth // wide, some, zero)

    def leave(field, which):
        copies = []
        for step in far_steps:
            peer = los_peer(step)
            copy = send(
                field.at[pl.ds(peer * planes, planes)], rb.at[which, los],
                out_send.at[which, step], out_recv.at[which, step], tr, peer,
            )
            copy.start()
            copies.append(copy)
        rb[which, los] = field[here]
        return copies

    for copy in entered_f:
        copy.wait_recv()
    dot_bz = solve(tf, zf)
    edge_rows(zf, 0)
    edge_columns(zf, 0)
    left_z = leave(zf, 0)
    operate_inside(zf, tf)
    edge_each(0, 0, "arrived")
    edge_each(0, 1, "arrived")
    dot_zq = operate_edges(zf, 0, qf)
    dot_qw = solve(qf, wf)
    edge_rows(wf, 1)
    edge_columns(wf, 1)
    left_q = leave(qf, 1)
    left_w = leave(wf, 2)
    operate_inside(wf, qf)
    edge_each(1, 0, "arrived")
    edge_each(1, 1, "arrived")
    dot_ws = operate_edges(wf, 1, vf)

    for n, dot in enumerate((dot_bz, dot_zq, dot_qw, dot_ws)):
        ps[0, n:n + 1, :] = jnp.sum(dot, axis=0, keepdims=True)
    summed = []
    for slot in range(n_tr - 1, 0, -1):
        copy = send(
            ps.at[0], p1.at[slot], sum_send.at[slot], sum_recv.at[slot], tr_peer(slot), los
        )
        copy.start()
        summed.append(copy)
    left_v = leave(vf, 3)
    total = ps[0]
    for copy in summed:
        copy.wait_recv()
    for slot in range(1, n_tr):
        total = total + p1[slot]
    ps[1] = total
    finals = []
    for step in far_steps:
        copy = send(
            ps.at[1], p2.at[step], fin_send.at[step], fin_recv.at[step], tr, los_peer(step)
        )
        copy.start()
        finals.append(copy)
    for copy in finals:
        copy.wait_recv()
    for step in range(1, n_los):
        total = total + p2[step]
    total = jnp.sum(total, axis=1, keepdims=True)
    bz, zq, qw, ws = (
        jnp.broadcast_to(total[n:n + 1], (8, 128)) for n in range(4)
    )
    alpha = bz / zq
    rz = alpha * alpha * qw - bz
    beta = rz / bz
    grown = 1.0 + beta
    alpha_next = rz / (grown * grown * zq - 2.0 * grown * alpha * qw + alpha * alpha * ws)
    main = alpha + alpha_next * grown
    other = alpha * alpha_next

    for copies in (left_z, left_w, left_q, left_v):
        for copy in copies:
            copy.wait_recv()

    def finish(k, none):
        for p in range(planes):
            x = main * rb[0, k, p] - other * rb[2, k, p]
            r = sf[k * planes + p] - main * rb[1, k, p] + other * rb[3, k, p]
            for part in range(2):
                at = pl.ds(pl.multiple_of(k * CHUNK + part * 128, 128), 128)
                sol_ref[p, :, at] = x[part * SX:(part + 1) * SX]
                res_ref[p, :, at] = r[part * SX:(part + 1) * SX]
        return none

    lax.fori_loop(0, n_los, finish, 0)

    for copies in (routed[0][1:], routed[1][1:], entered_w, entered_f,
                   left_z, left_q, left_w, left_v, summed, finals):
        for copy in copies:
            copy.wait_send()
    for turn in range(2):
        for kind in range(2):
            edge_each(turn, kind, "sent")


def local(flux, noise_weight, pixel_owner, pixel_cell, plane_bin, bin_coeffs):
    n_tr, n_los = lax.axis_size("tr"), lax.axis_size("los")
    nzr = 8 if n_tr == 32 else 2
    planes, pix = flux.shape
    depth = planes * n_los
    cols = n_los * CHUNK
    jump = min(8, n_tr)
    span = jump * CAP
    each = SX * planes
    dma = pltpu.SemaphoreType.DMA
    field = pltpu.VMEM((depth, 8, 128), F32)
    vmem = pl.BlockSpec(memory_space=pltpu.VMEM)
    hbm = pl.BlockSpec(memory_space=pltpu.MemorySpace.HBM)
    out = jax.ShapeDtypeStruct((planes, SX, cols), F32)
    return pl.pallas_call(
        functools.partial(kernel, n_tr, n_los, nzr),
        out_shape=(out, out),
        in_specs=[hbm] * 6,
        out_specs=(vmem, vmem),
        scratch_shapes=[
            pltpu.VMEM((planes, pix), F32), pltpu.VMEM((planes, pix), F32),
            pltpu.VMEM((1, pix), I32), pltpu.VMEM((1, pix), I32),
            pltpu.SMEM(plane_bin.shape, I32), pltpu.SMEM(bin_coeffs.shape, F32),
            pltpu.VMEM((2 * n_tr * (planes + 1), pix), BF16),
            pltpu.VMEM((2 * n_los * each, span), BF16),
            pltpu.VMEM((n_tr, planes + 1, CAP), F32),
            pltpu.VMEM((n_tr, planes, CAP), F32),
            pltpu.VMEM((n_tr, planes + 1, CAP), F32),
            pltpu.VMEM((n_tr, planes, CAP), F32),
            pltpu.VMEM((n_tr // jump, CHUNK, span), BF16),
            pltpu.VMEM((n_tr // jump, 16, span), BF16),
            pltpu.VMEM((n_los * each, CHUNK), F32),
            field, field, field, field,
            field, field, field, field, field, field, field, field, field, field, field,
            pltpu.VMEM((2, 2, depth // 4, 8, 128), F32),
            pltpu.VMEM((2, 2, depth // 4, 8, 128), F32),
            pltpu.VMEM((2, 8, 128), F32),
            pltpu.VMEM((2, 2, 8, 128), F32),
            pltpu.VMEM((4, n_los, planes, 8, 128), F32),
            pltpu.VMEM((2, 4, 128), F32),
            pltpu.VMEM((n_tr, 4, 128), F32),
            pltpu.VMEM((n_los, 4, 128), F32),
            dma((6,)), dma((2, n_tr)), dma((2, n_tr)), dma((2, n_los)), dma((2, n_los)),
            dma((2, 2, 2)), dma((2, 2, 2)), dma((4, n_los)), dma((4, n_los)),
            dma((n_tr,)), dma((n_tr,)), dma((n_los,)), dma((n_los,)),
        ],
        compiler_params=pltpu.CompilerParams(
            collective_id=0, has_side_effects=True, vmem_limit_bytes=50 * 1024 * 1024
        ),
        name="wiener",
    )(
        *(pltpu.with_memory_space_constraint(x, pltpu.MemorySpace.HBM) for x in (
            flux, noise_weight, pixel_owner.reshape(1, pix), pixel_cell.reshape(1, pix),
            plane_bin, bin_coeffs,
        ))
    )


def solution(mesh):
    placed = (P("los", "tr"), P("los", "tr"), P("tr", None), P("tr"), P(), P())
    return jax.shard_map(
        local,
        mesh=mesh,
        in_specs=placed,
        out_specs=(P("los", "tr", None), P("los", "tr", None)),
        check_vma=False,
    )
```

```python
import functools

import jax
import jax.numpy as jnp
from jax import lax
from jax.experimental import pallas as pl
from jax.experimental.pallas import tpu as pltpu
from jax.sharding import PartitionSpec as P

MESH = pl.DeviceIdType.MESH
F32 = jnp.float32
BF16 = jnp.bfloat16
I32 = jnp.int32
SX = 4
CHUNK = 256
CAP = 128
MASS = 0.5
NT = (((1,), (1,)), ((), ()))


def iota(shape, dim):
    return lax.broadcasted_iota(I32, shape, dim)


def two_pieces(values):
    high = values.astype(BF16)
    return high, (values - high.astype(F32)).astype(BF16)


def roll(x, shift, axis):
    size = x.shape[axis]
    return pltpu.roll(x, shift % size if isinstance(shift, int) else shift, axis)


def kernel(
    n_tr, n_los, nzr, flux_hbm, weight_hbm, owner_hbm, cell_hbm, bin_hbm, coef_hbm,
    sol_ref, res_ref,
    flux_ref, weight_ref, owner_ref, cell_ref, bin_ref, coef_ref,
    xp, hot_slot, xs, pw, pf, rw, rf, lows, dests, acc, sw, sf, tw, tf,
    kxs, kys, lks, base, inv, gf, zf, qf, wf, vf, pre,
    hs, hr, cs, cr, rb, ps, p1, p2,
    load_sem, route_send, route_recv, in_send, in_recv, halo_send, halo_recv,
    out_send, out_recv, sum_send, sum_recv, fin_send, fin_recv,
):
    planes, pix = flux_ref.shape
    depth = planes * n_los
    half = depth // 2
    groups = depth // 4
    tr = lax.axis_index("tr")
    los = lax.axis_index("los")
    nyr = n_tr // nzr
    y, zc = tr // nzr, tr % nzr
    offsets = [(dy, dz) for dy in range(nyr) for dz in range(nzr)]
    offsets.sort(key=lambda o: (min(o[0], nyr - o[0]) + min(o[1], nzr - o[1]), o))
    far_steps = sorted(range(1, n_los), key=lambda d: -min(d, n_los - d))

    ring_y = [((y + d) % nyr) * nzr for d in range(nyr)]
    ring_z = [(zc + d) % nzr for d in range(nzr)]
    ring_los = [(los + d) % n_los for d in range(n_los)]

    def tr_peer(slot):
        dy, dz = offsets[slot]
        return ring_y[dy] + ring_z[dz]

    def los_peer(step):
        return ring_los[step]

    def send(src, dst, ssem, rsem, at_tr, at_los):
        return pltpu.make_async_remote_copy(
            src_ref=src, dst_ref=dst, send_sem=ssem, recv_sem=rsem,
            device_id=(at_tr, at_los), device_id_type=MESH,
        )

    barrier = pltpu.get_barrier_semaphore()
    for slot in range(n_tr - 1, 0, -1):
        pl.semaphore_signal(barrier, inc=1, device_id=(tr_peer(slot), los), device_id_type=MESH)
    for step in far_steps:
        pl.semaphore_signal(barrier, inc=1, device_id=(tr, los_peer(step)), device_id_type=MESH)

    loads = [
        pltpu.make_async_copy(src, dst, load_sem.at[n])
        for n, (src, dst) in enumerate((
            (owner_hbm, owner_ref), (weight_hbm, weight_ref), (cell_hbm, cell_ref),
            (flux_hbm, flux_ref), (bin_hbm, bin_ref), (coef_hbm, coef_ref),
        ))
    ]
    for load in loads:
        load.start()

    @pl.when(tr == 0)
    def _():
        for turn in range(2):
            hr[turn, 0] = jnp.zeros_like(hr[turn, 0])

    @pl.when(tr == n_tr - 1)
    def _():
        for turn in range(2):
            hr[turn, 1] = jnp.zeros_like(hr[turn, 1])

    @pl.when(los == 0)
    def _():
        for turn in range(2):
            cr[turn, 0] = jnp.zeros_like(cr[turn, 0])

    @pl.when(los == n_los - 1)
    def _():
        for turn in range(2):
            cr[turn, 1] = jnp.zeros_like(cr[turn, 1])

    loads[0].wait()
    owner = owner_ref[...]
    hot = jnp.where(iota((n_tr, pix), 0) == owner, 1.0, 0.0).astype(F32)
    blk = min(256, pix)
    blocks = pix // blk
    stacked = jnp.concatenate(
        [hot[:, b * blk:(b + 1) * blk] for b in range(blocks)], axis=0
    ).astype(BF16)
    before = jnp.where(iota((blk, blk), 0) < iota((blk, blk), 1), 1.0, 0.0).astype(BF16)
    prefix = jnp.dot(stacked, before, preferred_element_type=F32)
    carry = jnp.zeros((n_tr, 1), F32)
    ranks = []
    for b in range(blocks):
        part = hot[:, b * blk:(b + 1) * blk]
        ranks.append(
            jnp.sum(part * (prefix[b * n_tr:(b + 1) * n_tr] + carry), axis=0, keepdims=True)
        )
        carry = carry + jnp.sum(part, axis=1, keepdims=True)
    rank = jnp.concatenate(ranks, axis=1)
    which = owner // 2
    one = jnp.ones((16, pix), BF16)
    nothing = jnp.zeros((16, pix), BF16)
    sub16 = iota((16, pix), 0)
    lanes = (
        jnp.broadcast_to(rank.astype(I32) + CAP * (owner - 2 * which), (16, pix)) - sub16
    ).astype(F32).astype(BF16)
    for t in range(0, 2 * CAP, 16):
        hot_slot[t:t + 16, :] = jnp.where(lanes == jnp.asarray(t, BF16), one, nothing)
    pair = 16 // planes
    which16 = jnp.broadcast_to(which, (16, pix))
    mine16 = (which16 - sub16 // planes).astype(F32).astype(BF16)
    rows = n_tr // 2 * planes

    def spread_by_owner(values, at):
        twice = jnp.concatenate([values] * pair, axis=0)
        for o in range(0, n_tr // 2, pair):
            xp[at + o * planes:at + (o + pair) * planes, :] = jnp.where(
                mine16 == jnp.asarray(o, BF16), twice, nothing
            )

    def pack(count):
        packed = lax.dot_general(
            xp[0:2 * count, :], hot_slot[...], NT, preferred_element_type=F32
        )
        return packed[0:count] + packed[count:2 * count]

    def of_owner(packed, o, at, height):
        return packed[at:at + height, (o % 2) * CAP:(o % 2 + 1) * CAP]

    for load in loads[1:]:
        load.wait()
    weight = weight_ref[...]
    wa, wb = two_pieces(weight)
    ca, cb = two_pieces(cell_ref[...].astype(F32))
    extra = rows + 16
    spread_by_owner(wa, 0)
    spread_by_owner(wb, extra)
    here16 = (which16 - sub16).astype(F32).astype(BF16) == jnp.asarray(0, BF16)
    xp[rows:extra, :] = jnp.where(here16, jnp.broadcast_to(ca, (16, pix)), nothing)
    xp[extra + rows:2 * extra, :] = jnp.where(here16, jnp.broadcast_to(cb, (16, pix)), nothing)
    packed = pack(extra)
    for o in range(n_tr):
        pw[o, 0:planes, :] = of_owner(packed, o, o // 2 * planes, planes)
        pw[o, planes:planes + 1, :] = of_owner(packed, o, rows + o // 2, 1)

    pl.semaphore_wait(barrier, n_tr - 1 + n_los - 1)

    routed = [None], [None]

    orders = (
        [*range(1, n_tr // 2), *range(n_tr - 1, n_tr // 2 - 1, -1)],
        [*range(1, n_tr // 4), *range(n_tr - 1, n_tr // 4 - 1, -1)],
    )

    def route(stage, packs, into):
        for slot in range(1, n_tr):
            peer = tr_peer(slot)
            routed[stage].append(send(
                packs.at[peer], into.at[slot],
                route_send.at[stage, slot], route_recv.at[stage, slot], peer, los,
            ))
        for slot in orders[stage]:
            routed[stage][slot].start()

    route(0, pw, rw)
    rw[0] = pw[tr]

    fa, fb = two_pieces(flux_ref[...] * weight)
    spread_by_owner(fa, 0)
    spread_by_owner(fb, rows)
    packed = pack(rows)
    for o in range(n_tr):
        pf[o] = of_owner(packed, o, o // 2 * planes, planes)
    route(1, pf, rf)
    rf[0] = pf[tr]

    def spread(zi, last):
        b = bin_ref[zi]
        kx = jnp.full((8, 128), coef_ref[0, b], F32)
        ky = jnp.full((8, 128), coef_ref[1, b], F32)
        link = jnp.full((8, 128), coef_ref[2, b], F32)
        link = jnp.where(zi < depth - 1, link, jnp.zeros_like(link))
        kxs[zi] = kx
        kys[zi] = ky
        lks[zi] = link
        base[zi] = MASS + 2.0 * kx + 2.0 * ky + (last + link)
        return link

    lax.fori_loop(0, depth, spread, jnp.zeros((8, 128), F32))

    width = n_los * CHUNK
    jump = min(8, n_tr)
    span = jump * CAP
    chunks = n_tr // jump
    each = SX * planes
    full = n_los * each
    upper = iota((8, span), 0) < SX
    sub_span = iota((16, span), 0)
    row16 = sub_span % SX
    ones = jnp.ones((16, span), BF16)
    none = jnp.zeros((16, span), BF16)
    upper3 = iota((planes // 2, 8, 128), 1) < SX

    def scatter(stage, g):
        arrived = (rw, rf)[stage]

        def build():
            slots = range(g * jump, (g + 1) * jump)
            if stage == 0:
                cell = jnp.concatenate([arrived[t, planes:planes + 1, :] for t in slots], axis=1)
                cell = (cell + 0.5).astype(I32)
                col = cell % width
                place = (col // CHUNK) * SX + cell // width
                low = (
                    jnp.broadcast_to(col % CHUNK, (16, span)) - sub_span
                ).astype(F32).astype(BF16)
                for t in range(0, CHUNK, 16):
                    lows[g, t:t + 16, :] = jnp.where(low == jnp.asarray(t, BF16), ones, none)
                dests[g] = (
                    jnp.broadcast_to(place, (16, span)) - row16
                ).astype(F32).astype(BF16)
            vals = jnp.concatenate([arrived[t, 0:planes, :] for t in slots], axis=1)
            ba, bb = two_pieces(jnp.concatenate([
                jnp.where(
                    upper,
                    jnp.broadcast_to(vals[p:p + 1], (8, span)),
                    jnp.broadcast_to(vals[p + 1:p + 2], (8, span)),
                )
                for p in range(0, planes, 2)
            ], axis=0))
            dest = dests[g]
            for k in range(n_los):
                mine = dest == jnp.asarray(SX * k, BF16)
                for t in range(0, each, 16):
                    at = k * each + t
                    xs[stage, at:at + 16, :] = jnp.where(mine, ba[t:t + 16], none)
                    xs[stage, full + at:full + at + 16, :] = jnp.where(mine, bb[t:t + 16], none)

        def add():
            part = lax.dot_general(xs[stage], lows[g], NT, preferred_element_type=F32)
            part = part[0:full] + part[full:2 * full]
            if g == 0:
                acc[stage] = part
            else:
                acc[stage] = acc[stage] + part

        for slot in range(g * jump, (g + 1) * jump):
            if slot:
                routed[stage][slot].wait_recv()
        build()
        add()

    here = pl.ds(los * planes, planes)

    def enter(stage, out, into):
        for k in range(n_los):
            both = acc[stage, k * each:(k + 1) * each, :]
            left = both[:, 0:128].reshape(planes // 2, 8, 128)
            right = both[:, 128:256].reshape(planes // 2, 8, 128)
            even = jnp.where(upper3, left, roll(right, 4, 1))
            odd = jnp.where(upper3, roll(left, 4, 1), right)
            for p in range(planes // 2):
                out[k * planes + 2 * p] = even[p]
                out[k * planes + 2 * p + 1] = odd[p]
        copies = []
        for step in far_steps:
            peer = los_peer(step)
            copy = send(
                out.at[pl.ds(peer * planes, planes)], into.at[here],
                in_send.at[stage, step], in_recv.at[stage, step], tr, peer,
            )
            copy.start()
            copies.append(copy)
        into[here] = out[here]
        return copies

    near = max(1, chunks // 2)
    for g in range(near):
        scatter(0, g)
    scatter(1, 0)
    for g in range(chunks - 1, near - 1, -1):
        scatter(0, g)
    entered_w = enter(0, sw, tw)
    for g in range(1, chunks):
        scatter(1, g)
    entered_f = enter(1, sf, tf)

    for copy in entered_w:
        copy.wait_recv()

    stride = min(8, half)
    zero = jnp.zeros((8, 128), F32)

    def pivots(block, state):
        it, lt, ib = state
        for u in range(stride):
            zt = block * stride + u
            zb = depth - 1 - zt
            it = 1.0 / ((base[zt] + tw[zt]) - (lt * lt) * it)
            lb = lks[zb]
            ib = 1.0 / ((base[zb] + tw[zb]) - (lb * lb) * ib)
            lt = lks[zt]
            inv[zt] = it
            inv[zb] = ib
        return it, lt, ib

    it, lt, ib = lax.fori_loop(0, half // stride, pivots, (zero,) * 3)
    ratio_top, ratio_bottom = lt * it, lt * ib
    middle = 1.0 / (1.0 - ratio_top * ratio_bottom)

    def solve(source, out):
        def eliminate(block, state):
            gt, lt, gb = state
            for u in range(stride):
                zt = block * stride + u
                zb = depth - 1 - zt
                gt = (source[zt] + lt * gt) * inv[zt]
                gb = (source[zb] + lks[zb] * gb) * inv[zb]
                lt = lks[zt]
                gf[zt] = gt
                gf[zb] = gb
            return gt, lt, gb

        gt, _, gb = lax.fori_loop(0, half // stride, eliminate, (zero,) * 3)
        yt = (gt + ratio_top * gb) * middle
        yb = gb + ratio_bottom * yt
        out[half - 1] = yt
        out[half] = yb
        total = source[half - 1] * yt + source[half] * yb

        def one(zt, state):
            yt, yb, total = state
            zb = depth - 1 - zt
            yt = gf[zt] + (lks[zt] * inv[zt]) * yt
            yb = gf[zb] + (lks[zb - 1] * inv[zb]) * yb
            out[zt] = yt
            out[zb] = yb
            return yt, yb, total + (source[zt] * yt + source[zb] * yb)

        state = (yt, yb, total)
        for u in range(stride - 1):
            state = one(half - 2 - u, state)

        def some(block, state):
            for u in range(stride):
                state = one(half - 1 - (block * stride + u), state)
            return state

        return lax.fori_loop(1, half // stride, some, state)[2]

    sub = iota((8, 128), 0)
    lane = iota((8, 128), 1)
    quarter = sub % 4
    first_row, last_row = quarter == 0, quarter == 3
    in_half = sub < 4
    inner_left, inner_right = (lane == 0) & ~in_half, (lane == 127) & in_half
    outer = ((lane == 0) & in_half) | ((lane == 127) & ~in_half)

    def edge_copy(turn, side, kind):
        step = 1 if side == 0 else -1
        if kind == 0:
            src, dst, where = hs.at[turn, side], hr.at[turn, side], (
                (tr + step + n_tr) % n_tr, los)
        else:
            src, dst, where = cs.at[turn], cr.at[turn, side], (tr, (los + step + n_los) % n_los)
        return send(
            src, dst, halo_send.at[turn, side, kind], halo_recv.at[turn, side, kind], *where
        )

    def edge_each(turn, kind, what):
        for side in range(2):
            copy = edge_copy(turn, side, kind)
            here_is, size = (tr, n_tr) if kind == 0 else (los, n_los)
            first, last = (0, size - 1) if side == 0 else (size - 1, 0)
            if what == "start":
                pl.when(here_is != last)(copy.start)
            elif what == "sent":
                pl.when(here_is != last)(copy.wait_send)
            else:
                pl.when(here_is != first)(copy.wait_recv)

    wide = min(32, depth)

    def edge_rows(field, turn):
        def pack(block, none):
            for i in range(wide // 4):
                down = up = zero
                for j in range(4):
                    v = field[block * wide + i * 4 + j]
                    down = jnp.where(quarter == j, roll(v, j - 3, 0), down)
                    up = jnp.where(quarter == j, roll(v, j, 0), up)
                hs[turn, 0, block * (wide // 4) + i] = down
                hs[turn, 1, block * (wide // 4) + i] = up
            return none

        lax.fori_loop(0, depth // wide, pack, 0)
        edge_each(turn, 0, "start")

    def edge_columns(field, turn):
        def pack(block, found):
            for i in range(wide):
                zi = block * wide + i
                u = roll(field[zi], 4, 0)
                both = jnp.where(in_half, roll(u, 1, 1), u)
                found = jnp.where(lane == zi, roll(both, zi, 1), found)
            return found

        cs[turn] = lax.fori_loop(0, depth // wide, pack, zero)
        edge_each(turn, 1, "start")

    def operate_inside(field, source):
        def some(block, none):
            for i in range(wide):
                zi = block * wide + i
                v = field[zi]
                u = roll(v, 4, 0)
                up = jnp.where(first_row, 0.0, roll(v, 1, 0))
                down = jnp.where(last_row, 0.0, roll(v, -1, 0))
                before = jnp.where(inner_left, roll(u, 1, 1), roll(v, 1, 1))
                after = jnp.where(inner_right, roll(u, 127, 1), roll(v, 127, 1))
                beside = jnp.where(in_half & (lane == 0), after, before + after)
                beside = jnp.where((lane == 127) & ~in_half, before, beside)
                pre[zi] = source[zi] - (kxs[zi] * (up + down) + kys[zi] * beside)
            return none

        lax.fori_loop(0, depth // wide, some, 0)

    def operate_edges(field, turn, out):
        columns = jnp.where(in_half, cr[turn, 0], roll(cr[turn, 1], 127, 1))

        def some(block, total):
            for i in range(wide):
                zi = block * wide + i
                j = i % 4
                four = block * (wide // 4) + i // 4
                above, below = hr[turn, 0, four], hr[turn, 1, four]
                rows = jnp.where(
                    first_row, roll(above, -j, 0), jnp.where(last_row, roll(below, 3 - j, 0), 0.0)
                )
                beside = jnp.where(outer, roll(columns, 128 - zi, 1), 0.0)
                image = pre[zi] - (kxs[zi] * rows + kys[zi] * beside)
                out[zi] = image
                total = total + field[zi] * image
            return total

        return lax.fori_loop(0, depth // wide, some, zero)

    def leave(field, which):
        copies = []
        for step in far_steps:
            peer = los_peer(step)
            copy = send(
                field.at[pl.ds(peer * planes, planes)], rb.at[which, los],
                out_send.at[which, step], out_recv.at[which, step], tr, peer,
            )
            copy.start()
            copies.append(copy)
        rb[which, los] = field[here]
        return copies

    for copy in entered_f:
        copy.wait_recv()
    dot_bz = solve(tf, zf)
    edge_rows(zf, 0)
    edge_columns(zf, 0)
    operate_inside(zf, tf)
    left_z = leave(zf, 0)
    edge_each(0, 0, "arrived")
    edge_each(0, 1, "arrived")
    dot_zq = operate_edges(zf, 0, qf)
    dot_qw = solve(qf, wf)
    edge_rows(wf, 1)
    edge_columns(wf, 1)
    operate_inside(wf, qf)
    left_q = leave(qf, 1)
    left_w = leave(wf, 2)
    edge_each(1, 0, "arrived")
    edge_each(1, 1, "arrived")
    dot_ws = operate_edges(wf, 1, vf)

    for n, dot in enumerate((dot_bz, dot_zq, dot_qw, dot_ws)):
        ps[0, n:n + 1, :] = jnp.sum(dot, axis=0, keepdims=True)
    summed = []
    for slot in range(n_tr - 1, 0, -1):
        copy = send(
            ps.at[0], p1.at[slot], sum_send.at[slot], sum_recv.at[slot], tr_peer(slot), los
        )
        copy.start()
        summed.append(copy)
    left_v = leave(vf, 3)
    total = ps[0]
    for copy in summed:
        copy.wait_recv()
    for slot in range(1, n_tr):
        total = total + p1[slot]
    ps[1] = total
    finals = []
    for step in far_steps:
        copy = send(
            ps.at[1], p2.at[step], fin_send.at[step], fin_recv.at[step], tr, los_peer(step)
        )
        copy.start()
        finals.append(copy)
    for copy in finals:
        copy.wait_recv()
    for step in range(1, n_los):
        total = total + p2[step]
    total = jnp.sum(total, axis=1, keepdims=True)
    bz, zq, qw, ws = (
        jnp.broadcast_to(total[n:n + 1], (8, 128)) for n in range(4)
    )
    alpha = bz / zq
    rz = alpha * alpha * qw - bz
    beta = rz / bz
    grown = 1.0 + beta
    alpha_next = rz / (grown * grown * zq - 2.0 * grown * alpha * qw + alpha * alpha * ws)
    main = alpha + alpha_next * grown
    other = alpha * alpha_next

    for copies in (left_z, left_w, left_q, left_v):
        for copy in copies:
            copy.wait_recv()

    def finish(k, none):
        for p in range(planes):
            x = main * rb[0, k, p] - other * rb[2, k, p]
            r = sf[k * planes + p] - main * rb[1, k, p] + other * rb[3, k, p]
            for part in range(2):
                at = pl.ds(pl.multiple_of(k * CHUNK + part * 128, 128), 128)
                sol_ref[p, :, at] = x[part * SX:(part + 1) * SX]
                res_ref[p, :, at] = r[part * SX:(part + 1) * SX]
        return none

    lax.fori_loop(0, n_los, finish, 0)

    for copies in (routed[0][1:], routed[1][1:], entered_w, entered_f,
                   left_z, left_q, left_w, left_v, summed, finals):
        for copy in copies:
            copy.wait_send()
    for turn in range(2):
        for kind in range(2):
            edge_each(turn, kind, "sent")


def local(flux, noise_weight, pixel_owner, pixel_cell, plane_bin, bin_coeffs):
    n_tr, n_los = lax.axis_size("tr"), lax.axis_size("los")
    nzr = 8 if n_tr == 32 else 2
    planes, pix = flux.shape
    depth = planes * n_los
    cols = n_los * CHUNK
    jump = min(8, n_tr)
    span = jump * CAP
    each = SX * planes
    dma = pltpu.SemaphoreType.DMA
    field = pltpu.VMEM((depth, 8, 128), F32)
    vmem = pl.BlockSpec(memory_space=pltpu.VMEM)
    hbm = pl.BlockSpec(memory_space=pltpu.MemorySpace.HBM)
    out = jax.ShapeDtypeStruct((planes, SX, cols), F32)
    return pl.pallas_call(
        functools.partial(kernel, n_tr, n_los, nzr),
        out_shape=(out, out),
        in_specs=[hbm] * 6,
        out_specs=(vmem, vmem),
        scratch_shapes=[
            pltpu.VMEM((planes, pix), F32), pltpu.VMEM((planes, pix), F32),
            pltpu.VMEM((1, pix), I32), pltpu.VMEM((1, pix), I32),
            pltpu.SMEM(plane_bin.shape, I32), pltpu.SMEM(bin_coeffs.shape, F32),
            pltpu.VMEM((2 * (n_tr // 2 * planes + 16), pix), BF16),
            pltpu.VMEM((2 * CAP, pix), BF16),
            pltpu.VMEM((2, 2 * n_los * each, span), BF16),
            pltpu.VMEM((n_tr, planes + 1, CAP), F32),
            pltpu.VMEM((n_tr, planes, CAP), F32),
            pltpu.VMEM((n_tr, planes + 1, CAP), F32),
            pltpu.VMEM((n_tr, planes, CAP), F32),
            pltpu.VMEM((n_tr // jump, CHUNK, span), BF16),
            pltpu.VMEM((n_tr // jump, 16, span), BF16),
            pltpu.VMEM((2, n_los * each, CHUNK), F32),
            field, field, field, field,
            field, field, field, field, field, field, field, field, field, field, field,
            pltpu.VMEM((2, 2, depth // 4, 8, 128), F32),
            pltpu.VMEM((2, 2, depth // 4, 8, 128), F32),
            pltpu.VMEM((2, 8, 128), F32),
            pltpu.VMEM((2, 2, 8, 128), F32),
            pltpu.VMEM((4, n_los, planes, 8, 128), F32),
            pltpu.VMEM((2, 4, 128), F32),
            pltpu.VMEM((n_tr, 4, 128), F32),
            pltpu.VMEM((n_los, 4, 128), F32),
            dma((6,)), dma((2, n_tr)), dma((2, n_tr)), dma((2, n_los)), dma((2, n_los)),
            dma((2, 2, 2)), dma((2, 2, 2)), dma((4, n_los)), dma((4, n_los)),
            dma((n_tr,)), dma((n_tr,)), dma((n_los,)), dma((n_los,)),
        ],
        compiler_params=pltpu.CompilerParams(
            collective_id=0, has_side_effects=True, vmem_limit_bytes=50 * 1024 * 1024
        ),
        name="wiener",
    )(
        *(pltpu.with_memory_space_constraint(x, pltpu.MemorySpace.HBM) for x in (
            flux, noise_weight, pixel_owner.reshape(1, pix), pixel_cell.reshape(1, pix),
            plane_bin, bin_coeffs,
        ))
    )


def solution(mesh):
    placed = (P("los", "tr"), P("los", "tr"), P("tr", None), P("tr"), P(), P())
    return jax.shard_map(
        local,
        mesh=mesh,
        in_specs=placed,
        out_specs=(P("los", "tr", None), P("los", "tr", None)),
        check_vma=False,
    )
```

```python
import functools

import jax
import jax.numpy as jnp
from jax import lax
from jax.experimental import pallas as pl
from jax.experimental.pallas import tpu as pltpu
from jax.sharding import PartitionSpec as P

MESH = pl.DeviceIdType.MESH
F32 = jnp.float32
BF16 = jnp.bfloat16
I32 = jnp.int32
SX = 4
CHUNK = 256
CAP = 128
MASS = 0.5
NT = (((1,), (1,)), ((), ()))


def iota(shape, dim):
    return lax.broadcasted_iota(I32, shape, dim)


def two_pieces(values):
    high = values.astype(BF16)
    return high, (values - high.astype(F32)).astype(BF16)


def roll(x, shift, axis):
    size = x.shape[axis]
    return pltpu.roll(x, shift % size if isinstance(shift, int) else shift, axis)


def kernel(
    n_tr, n_los, nzr, flux_hbm, weight_hbm, owner_hbm, cell_hbm, bin_hbm, coef_hbm,
    rb, sf, factors,
    flux_ref, weight_ref, owner_ref, cell_ref, bin_ref, coef_ref,
    xp, hot_slot, xs, pw, pf, rw, rf, lows, dests, acc, sw, tw, tf,
    kxs, kys, lks, base, inv, gf, zf, qf, wf, vf, pre,
    hs, hr, cs, cr, ps, p1, p2,
    load_sem, route_send, route_recv, in_send, in_recv, halo_send, halo_recv,
    out_send, out_recv, sum_send, sum_recv, fin_send, fin_recv,
):
    planes, pix = flux_ref.shape
    depth = planes * n_los
    half = depth // 2
    groups = depth // 4
    tr = lax.axis_index("tr")
    los = lax.axis_index("los")
    nyr = n_tr // nzr
    y, zc = tr // nzr, tr % nzr
    offsets = [(dy, dz) for dy in range(nyr) for dz in range(nzr)]
    offsets.sort(key=lambda o: (min(o[0], nyr - o[0]) + min(o[1], nzr - o[1]), o))
    far_steps = sorted(range(1, n_los), key=lambda d: -min(d, n_los - d))

    ring_y = [((y + d) % nyr) * nzr for d in range(nyr)]
    ring_z = [(zc + d) % nzr for d in range(nzr)]
    ring_los = [(los + d) % n_los for d in range(n_los)]

    def tr_peer(slot):
        dy, dz = offsets[slot]
        return ring_y[dy] + ring_z[dz]

    def los_peer(step):
        return ring_los[step]

    def send(src, dst, ssem, rsem, at_tr, at_los):
        return pltpu.make_async_remote_copy(
            src_ref=src, dst_ref=dst, send_sem=ssem, recv_sem=rsem,
            device_id=(at_tr, at_los), device_id_type=MESH,
        )

    barrier = pltpu.get_barrier_semaphore()
    for slot in range(n_tr - 1, 0, -1):
        pl.semaphore_signal(barrier, inc=1, device_id=(tr_peer(slot), los), device_id_type=MESH)
    for step in far_steps:
        pl.semaphore_signal(barrier, inc=1, device_id=(tr, los_peer(step)), device_id_type=MESH)

    loads = [
        pltpu.make_async_copy(src, dst, load_sem.at[n])
        for n, (src, dst) in enumerate((
            (owner_hbm, owner_ref), (weight_hbm, weight_ref), (cell_hbm, cell_ref),
            (flux_hbm, flux_ref), (bin_hbm, bin_ref), (coef_hbm, coef_ref),
        ))
    ]
    for load in loads:
        load.start()

    @pl.when(tr == 0)
    def _():
        for turn in range(2):
            hr[turn, 0] = jnp.zeros_like(hr[turn, 0])

    @pl.when(tr == n_tr - 1)
    def _():
        for turn in range(2):
            hr[turn, 1] = jnp.zeros_like(hr[turn, 1])

    @pl.when(los == 0)
    def _():
        for turn in range(2):
            cr[turn, 0] = jnp.zeros_like(cr[turn, 0])

    @pl.when(los == n_los - 1)
    def _():
        for turn in range(2):
            cr[turn, 1] = jnp.zeros_like(cr[turn, 1])

    loads[0].wait()
    owner = owner_ref[...]
    hot = jnp.where(iota((n_tr, pix), 0) == owner, 1.0, 0.0).astype(F32)
    blk = min(256, pix)
    blocks = pix // blk
    stacked = jnp.concatenate(
        [hot[:, b * blk:(b + 1) * blk] for b in range(blocks)], axis=0
    ).astype(BF16)
    before = jnp.where(iota((blk, blk), 0) < iota((blk, blk), 1), 1.0, 0.0).astype(BF16)
    prefix = jnp.dot(stacked, before, preferred_element_type=F32)
    carry = jnp.zeros((n_tr, 1), F32)
    ranks = []
    for b in range(blocks):
        part = hot[:, b * blk:(b + 1) * blk]
        ranks.append(
            jnp.sum(part * (prefix[b * n_tr:(b + 1) * n_tr] + carry), axis=0, keepdims=True)
        )
        carry = carry + jnp.sum(part, axis=1, keepdims=True)
    rank = jnp.concatenate(ranks, axis=1)
    which = owner // 2
    one = jnp.ones((16, pix), BF16)
    nothing = jnp.zeros((16, pix), BF16)
    sub16 = iota((16, pix), 0)
    lanes = (
        jnp.broadcast_to(rank.astype(I32) + CAP * (owner - 2 * which), (16, pix)) - sub16
    ).astype(F32).astype(BF16)
    for t in range(0, 2 * CAP, 16):
        hot_slot[t:t + 16, :] = jnp.where(lanes == jnp.asarray(t, BF16), one, nothing)
    pair = 16 // planes
    which16 = jnp.broadcast_to(which, (16, pix))
    mine16 = (which16 - sub16 // planes).astype(F32).astype(BF16)
    rows = n_tr // 2 * planes

    def spread_by_owner(values, at):
        twice = jnp.concatenate([values] * pair, axis=0)
        for o in range(0, n_tr // 2, pair):
            xp[at + o * planes:at + (o + pair) * planes, :] = jnp.where(
                mine16 == jnp.asarray(o, BF16), twice, nothing
            )

    def pack(count):
        packed = lax.dot_general(
            xp[0:2 * count, :], hot_slot[...], NT, preferred_element_type=F32
        )
        return packed[0:count] + packed[count:2 * count]

    def of_owner(packed, o, at, height):
        return packed[at:at + height, (o % 2) * CAP:(o % 2 + 1) * CAP]

    for load in loads[1:]:
        load.wait()
    weight = weight_ref[...]
    wa, wb = two_pieces(weight)
    ca, cb = two_pieces(cell_ref[...].astype(F32))
    extra = rows + 16
    spread_by_owner(wa, 0)
    spread_by_owner(wb, extra)
    here16 = (which16 - sub16).astype(F32).astype(BF16) == jnp.asarray(0, BF16)
    xp[rows:extra, :] = jnp.where(here16, jnp.broadcast_to(ca, (16, pix)), nothing)
    xp[extra + rows:2 * extra, :] = jnp.where(here16, jnp.broadcast_to(cb, (16, pix)), nothing)
    packed = pack(extra)
    for o in range(n_tr):
        pw[o, 0:planes, :] = of_owner(packed, o, o // 2 * planes, planes)
        pw[o, planes:planes + 1, :] = of_owner(packed, o, rows + o // 2, 1)

    pl.semaphore_wait(barrier, n_tr - 1 + n_los - 1)

    routed = [None], [None]

    orders = (
        [*range(1, n_tr // 2), *range(n_tr - 1, n_tr // 2 - 1, -1)],
        [*range(1, n_tr // 4), *range(n_tr - 1, n_tr // 4 - 1, -1)],
    )

    def route(stage, packs, into):
        for slot in range(1, n_tr):
            peer = tr_peer(slot)
            routed[stage].append(send(
                packs.at[peer], into.at[slot],
                route_send.at[stage, slot], route_recv.at[stage, slot], peer, los,
            ))
        for slot in orders[stage]:
            routed[stage][slot].start()

    route(0, pw, rw)
    rw[0] = pw[tr]

    fa, fb = two_pieces(flux_ref[...] * weight)
    spread_by_owner(fa, 0)
    spread_by_owner(fb, rows)
    packed = pack(rows)
    for o in range(n_tr):
        pf[o] = of_owner(packed, o, o // 2 * planes, planes)
    route(1, pf, rf)
    rf[0] = pf[tr]

    def spread(zi, last):
        b = bin_ref[zi]
        kx = jnp.full((8, 128), coef_ref[0, b], F32)
        ky = jnp.full((8, 128), coef_ref[1, b], F32)
        link = jnp.full((8, 128), coef_ref[2, b], F32)
        link = jnp.where(zi < depth - 1, link, jnp.zeros_like(link))
        kxs[zi] = kx
        kys[zi] = ky
        lks[zi] = link
        base[zi] = MASS + 2.0 * kx + 2.0 * ky + (last + link)
        return link

    lax.fori_loop(0, depth, spread, jnp.zeros((8, 128), F32))

    width = n_los * CHUNK
    jump = min(8, n_tr)
    span = jump * CAP
    chunks = n_tr // jump
    each = SX * planes
    full = n_los * each
    upper = iota((8, span), 0) < SX
    sub_span = iota((16, span), 0)
    row16 = sub_span % SX
    ones = jnp.ones((16, span), BF16)
    none = jnp.zeros((16, span), BF16)
    upper3 = iota((planes // 2, 8, 128), 1) < SX

    def scatter(stage, g):
        arrived = (rw, rf)[stage]

        def build():
            slots = range(g * jump, (g + 1) * jump)
            if stage == 0:
                cell = jnp.concatenate([arrived[t, planes:planes + 1, :] for t in slots], axis=1)
                cell = (cell + 0.5).astype(I32)
                col = cell % width
                place = (col // CHUNK) * SX + cell // width
                low = (
                    jnp.broadcast_to(col % CHUNK, (16, span)) - sub_span
                ).astype(F32).astype(BF16)
                for t in range(0, CHUNK, 16):
                    lows[g, t:t + 16, :] = jnp.where(low == jnp.asarray(t, BF16), ones, none)
                dests[g] = (
                    jnp.broadcast_to(place, (16, span)) - row16
                ).astype(F32).astype(BF16)
            vals = jnp.concatenate([arrived[t, 0:planes, :] for t in slots], axis=1)
            ba, bb = two_pieces(jnp.concatenate([
                jnp.where(
                    upper,
                    jnp.broadcast_to(vals[p:p + 1], (8, span)),
                    jnp.broadcast_to(vals[p + 1:p + 2], (8, span)),
                )
                for p in range(0, planes, 2)
            ], axis=0))
            dest = dests[g]
            for k in range(n_los):
                mine = dest == jnp.asarray(SX * k, BF16)
                for t in range(0, each, 16):
                    at = k * each + t
                    xs[stage, at:at + 16, :] = jnp.where(mine, ba[t:t + 16], none)
                    xs[stage, full + at:full + at + 16, :] = jnp.where(mine, bb[t:t + 16], none)

        def add():
            part = lax.dot_general(xs[stage], lows[g], NT, preferred_element_type=F32)
            part = part[0:full] + part[full:2 * full]
            if g == 0:
                acc[stage] = part
            else:
                acc[stage] = acc[stage] + part

        for slot in range(g * jump, (g + 1) * jump):
            if slot:
                routed[stage][slot].wait_recv()
        build()
        add()

    here = pl.ds(los * planes, planes)

    def enter(stage, out, into):
        for k in range(n_los):
            both = acc[stage, k * each:(k + 1) * each, :]
            left = both[:, 0:128].reshape(planes // 2, 8, 128)
            right = both[:, 128:256].reshape(planes // 2, 8, 128)
            even = jnp.where(upper3, left, roll(right, 4, 1))
            odd = jnp.where(upper3, roll(left, 4, 1), right)
            for p in range(planes // 2):
                out[k * planes + 2 * p] = even[p]
                out[k * planes + 2 * p + 1] = odd[p]
        copies = []
        for step in far_steps:
            peer = los_peer(step)
            copy = send(
                out.at[pl.ds(peer * planes, planes)], into.at[here],
                in_send.at[stage, step], in_recv.at[stage, step], tr, peer,
            )
            copy.start()
            copies.append(copy)
        into[here] = out[here]
        return copies

    near = max(1, chunks // 2)
    for g in (*range(near), *range(chunks - 1, near - 1, -1)):
        scatter(0, g)
    entered_w = enter(0, sw, tw)
    for g in range(chunks):
        scatter(1, g)
    entered_f = enter(1, sf, tf)

    for copy in entered_w:
        copy.wait_recv()

    stride = min(8, half)
    zero = jnp.zeros((8, 128), F32)

    def pivots(block, state):
        it, lt, ib = state
        for u in range(stride):
            zt = block * stride + u
            zb = depth - 1 - zt
            it = 1.0 / ((base[zt] + tw[zt]) - (lt * lt) * it)
            lb = lks[zb]
            ib = 1.0 / ((base[zb] + tw[zb]) - (lb * lb) * ib)
            lt = lks[zt]
            inv[zt] = it
            inv[zb] = ib
        return it, lt, ib

    it, lt, ib = lax.fori_loop(0, half // stride, pivots, (zero,) * 3)
    ratio_top, ratio_bottom = lt * it, lt * ib
    middle = 1.0 / (1.0 - ratio_top * ratio_bottom)

    def solve(source, out):
        def eliminate(block, state):
            gt, lt, gb = state
            for u in range(stride):
                zt = block * stride + u
                zb = depth - 1 - zt
                gt = (source[zt] + lt * gt) * inv[zt]
                gb = (source[zb] + lks[zb] * gb) * inv[zb]
                lt = lks[zt]
                gf[zt] = gt
                gf[zb] = gb
            return gt, lt, gb

        gt, _, gb = lax.fori_loop(0, half // stride, eliminate, (zero,) * 3)
        yt = (gt + ratio_top * gb) * middle
        yb = gb + ratio_bottom * yt
        out[half - 1] = yt
        out[half] = yb
        total = source[half - 1] * yt + source[half] * yb

        def one(zt, state):
            yt, yb, total = state
            zb = depth - 1 - zt
            yt = gf[zt] + (lks[zt] * inv[zt]) * yt
            yb = gf[zb] + (lks[zb - 1] * inv[zb]) * yb
            out[zt] = yt
            out[zb] = yb
            return yt, yb, total + (source[zt] * yt + source[zb] * yb)

        state = (yt, yb, total)
        for u in range(stride - 1):
            state = one(half - 2 - u, state)

        def some(block, state):
            for u in range(stride):
                state = one(half - 1 - (block * stride + u), state)
            return state

        return lax.fori_loop(1, half // stride, some, state)[2]

    sub = iota((8, 128), 0)
    lane = iota((8, 128), 1)
    quarter = sub % 4
    first_row, last_row = quarter == 0, quarter == 3
    in_half = sub < 4
    inner_left, inner_right = (lane == 0) & ~in_half, (lane == 127) & in_half
    outer = ((lane == 0) & in_half) | ((lane == 127) & ~in_half)

    def edge_copy(turn, side, kind):
        step = 1 if side == 0 else -1
        if kind == 0:
            src, dst, where = hs.at[turn, side], hr.at[turn, side], (
                (tr + step + n_tr) % n_tr, los)
        else:
            src, dst, where = cs.at[turn], cr.at[turn, side], (tr, (los + step + n_los) % n_los)
        return send(
            src, dst, halo_send.at[turn, side, kind], halo_recv.at[turn, side, kind], *where
        )

    def edge_each(turn, kind, what):
        for side in range(2):
            copy = edge_copy(turn, side, kind)
            here_is, size = (tr, n_tr) if kind == 0 else (los, n_los)
            first, last = (0, size - 1) if side == 0 else (size - 1, 0)
            if what == "start":
                pl.when(here_is != last)(copy.start)
            elif what == "sent":
                pl.when(here_is != last)(copy.wait_send)
            else:
                pl.when(here_is != first)(copy.wait_recv)

    wide = min(32, depth)

    def edge_rows(field, turn):
        def pack(block, none):
            for i in range(wide // 4):
                down = up = zero
                for j in range(4):
                    v = field[block * wide + i * 4 + j]
                    down = jnp.where(quarter == j, roll(v, j - 3, 0), down)
                    up = jnp.where(quarter == j, roll(v, j, 0), up)
                hs[turn, 0, block * (wide // 4) + i] = down
                hs[turn, 1, block * (wide // 4) + i] = up
            return none

        lax.fori_loop(0, depth // wide, pack, 0)
        edge_each(turn, 0, "start")

    def edge_columns(field, turn):
        def pack(block, found):
            for i in range(wide):
                zi = block * wide + i
                u = roll(field[zi], 4, 0)
                both = jnp.where(in_half, roll(u, 1, 1), u)
                found = jnp.where(lane == zi, roll(both, zi, 1), found)
            return found

        cs[turn] = lax.fori_loop(0, depth // wide, pack, zero)
        edge_each(turn, 1, "start")

    def operate_inside(field, source):
        def some(block, none):
            for i in range(wide):
                zi = block * wide + i
                v = field[zi]
                u = roll(v, 4, 0)
                up = jnp.where(first_row, 0.0, roll(v, 1, 0))
                down = jnp.where(last_row, 0.0, roll(v, -1, 0))
                before = jnp.where(inner_left, roll(u, 1, 1), roll(v, 1, 1))
                after = jnp.where(inner_right, roll(u, 127, 1), roll(v, 127, 1))
                beside = jnp.where(in_half & (lane == 0), after, before + after)
                beside = jnp.where((lane == 127) & ~in_half, before, beside)
                pre[zi] = source[zi] - (kxs[zi] * (up + down) + kys[zi] * beside)
            return none

        lax.fori_loop(0, depth // wide, some, 0)

    def operate_edges(field, turn, out):
        columns = jnp.where(in_half, cr[turn, 0], roll(cr[turn, 1], 127, 1))

        def some(block, total):
            for i in range(wide):
                zi = block * wide + i
                j = i % 4
                four = block * (wide // 4) + i // 4
                above, below = hr[turn, 0, four], hr[turn, 1, four]
                rows = jnp.where(
                    first_row, roll(above, -j, 0), jnp.where(last_row, roll(below, 3 - j, 0), 0.0)
                )
                beside = jnp.where(outer, roll(columns, 128 - zi, 1), 0.0)
                image = pre[zi] - (kxs[zi] * rows + kys[zi] * beside)
                out[zi] = image
                total = total + field[zi] * image
            return total

        return lax.fori_loop(0, depth // wide, some, zero)

    def leave(field, which):
        copies = []
        for step in far_steps:
            peer = los_peer(step)
            copy = send(
                field.at[pl.ds(peer * planes, planes)], rb.at[which, los],
                out_send.at[which, step], out_recv.at[which, step], tr, peer,
            )
            copy.start()
            copies.append(copy)
        rb[which, los] = field[here]
        return copies

    for copy in entered_f:
        copy.wait_recv()
    dot_bz = solve(tf, zf)
    edge_rows(zf, 0)
    edge_columns(zf, 0)
    operate_inside(zf, tf)
    left_z = leave(zf, 0)
    edge_each(0, 0, "arrived")
    edge_each(0, 1, "arrived")
    dot_zq = operate_edges(zf, 0, qf)
    dot_qw = solve(qf, wf)
    edge_rows(wf, 1)
    edge_columns(wf, 1)
    operate_inside(wf, qf)
    left_q = leave(qf, 1)
    left_w = leave(wf, 2)
    edge_each(1, 0, "arrived")
    edge_each(1, 1, "arrived")
    dot_ws = operate_edges(wf, 1, vf)

    mixed = jnp.zeros((1, 128), F32)
    lane1 = iota((1, 128), 1) // 32
    for n, dot in enumerate((dot_bz, dot_zq, dot_qw, dot_ws)):
        row = jnp.sum(dot, axis=0, keepdims=True)
        row = row + roll(row, 64, 1)
        row = row + roll(row, 32, 1)
        mixed = jnp.where(lane1 == n, row, mixed)
    ps[0] = mixed
    summed = []
    for slot in range(n_tr - 1, 0, -1):
        copy = send(
            ps.at[0], p1.at[slot], sum_send.at[slot], sum_recv.at[slot], tr_peer(slot), los
        )
        copy.start()
        summed.append(copy)
    left_v = leave(vf, 3)
    total = ps[0]
    for copies in (routed[0][1:], routed[1][1:], entered_w, entered_f, left_z):
        for copy in copies:
            copy.wait_send()
    for turn in range(2):
        for kind in range(2):
            edge_each(turn, kind, "sent")
    for copy in summed:
        copy.wait_recv()
    for slot in range(1, n_tr):
        total = total + p1[slot]
    ps[1] = total
    finals = []
    for step in far_steps:
        copy = send(
            ps.at[1], p2.at[step], fin_send.at[step], fin_recv.at[step], tr, los_peer(step)
        )
        copy.start()
        finals.append(copy)
    for copy in finals:
        copy.wait_recv()
    for step in range(1, n_los):
        total = total + p2[step]
    bz, zq, qw, ws = (
        jnp.broadcast_to(
            jnp.sum(jnp.where(lane1 == n, total, 0.0), axis=1, keepdims=True), (8, 128)
        )
        for n in range(4)
    )
    alpha = bz / zq
    rz = alpha * alpha * qw - bz
    beta = rz / bz
    grown = 1.0 + beta
    alpha_next = rz / (grown * grown * zq - 2.0 * grown * alpha * qw + alpha * alpha * ws)
    main = alpha + alpha_next * grown
    other = alpha * alpha_next

    for copies in (left_z, left_w, left_q, left_v):
        for copy in copies:
            copy.wait_recv()

    factors[0] = main
    factors[1] = other

    for copies in (left_q, left_w, left_v, summed, finals):
        for copy in copies:
            copy.wait_send()


def finish(rb, bf, factors, sol_ref, res_ref):
    main, other = factors[0], factors[1]
    n_los, planes = rb.shape[1:3]
    for k in range(n_los):
        for p in range(planes):
            x = main * rb[0, k, p] - other * rb[2, k, p]
            r = bf[k * planes + p] - main * rb[1, k, p] + other * rb[3, k, p]
            for part in range(2):
                at = slice(k * CHUNK + part * 128, k * CHUNK + part * 128 + 128)
                sol_ref[p, :, at] = x[part * SX:(part + 1) * SX]
                res_ref[p, :, at] = r[part * SX:(part + 1) * SX]


def local(flux, noise_weight, pixel_owner, pixel_cell, plane_bin, bin_coeffs):
    n_tr, n_los = lax.axis_size("tr"), lax.axis_size("los")
    nzr = 8 if n_tr == 32 else 2
    planes, pix = flux.shape
    depth = planes * n_los
    cols = n_los * CHUNK
    jump = min(8, n_tr)
    span = jump * CAP
    each = SX * planes
    dma = pltpu.SemaphoreType.DMA
    field = pltpu.VMEM((depth, 8, 128), F32)
    vmem = pl.BlockSpec(memory_space=pltpu.VMEM)
    hbm = pl.BlockSpec(memory_space=pltpu.MemorySpace.HBM)
    out = jax.ShapeDtypeStruct((planes, SX, cols), F32)
    fields, right_side, factors = pl.pallas_call(
        functools.partial(kernel, n_tr, n_los, nzr),
        out_shape=(
            jax.ShapeDtypeStruct((4, n_los, planes, 8, 128), F32),
            jax.ShapeDtypeStruct((depth, 8, 128), F32),
            jax.ShapeDtypeStruct((2, 8, 128), F32),
        ),
        in_specs=[hbm] * 6,
        out_specs=(vmem, vmem, vmem),
        scratch_shapes=[
            pltpu.VMEM((planes, pix), F32), pltpu.VMEM((planes, pix), F32),
            pltpu.VMEM((1, pix), I32), pltpu.VMEM((1, pix), I32),
            pltpu.SMEM(plane_bin.shape, I32), pltpu.SMEM(bin_coeffs.shape, F32),
            pltpu.VMEM((2 * (n_tr // 2 * planes + 16), pix), BF16),
            pltpu.VMEM((2 * CAP, pix), BF16),
            pltpu.VMEM((2, 2 * n_los * each, span), BF16),
            pltpu.VMEM((n_tr, planes + 1, CAP), F32),
            pltpu.VMEM((n_tr, planes, CAP), F32),
            pltpu.VMEM((n_tr, planes + 1, CAP), F32),
            pltpu.VMEM((n_tr, planes, CAP), F32),
            pltpu.VMEM((n_tr // jump, CHUNK, span), BF16),
            pltpu.VMEM((n_tr // jump, 16, span), BF16),
            pltpu.VMEM((2, n_los * each, CHUNK), F32),
            field, field, field,
            field, field, field, field, field, field, field, field, field, field, field,
            pltpu.VMEM((2, 2, depth // 4, 8, 128), F32),
            pltpu.VMEM((2, 2, depth // 4, 8, 128), F32),
            pltpu.VMEM((2, 8, 128), F32),
            pltpu.VMEM((2, 2, 8, 128), F32),
            pltpu.VMEM((2, 1, 128), F32),
            pltpu.VMEM((n_tr, 1, 128), F32),
            pltpu.VMEM((n_los, 1, 128), F32),
            dma((6,)), dma((2, n_tr)), dma((2, n_tr)), dma((2, n_los)), dma((2, n_los)),
            dma((2, 2, 2)), dma((2, 2, 2)), dma((4, n_los)), dma((4, n_los)),
            dma((n_tr,)), dma((n_tr,)), dma((n_los,)), dma((n_los,)),
        ],
        compiler_params=pltpu.CompilerParams(
            collective_id=0, has_side_effects=True, vmem_limit_bytes=50 * 1024 * 1024
        ),
        name="wiener",
    )(
        *(pltpu.with_memory_space_constraint(x, pltpu.MemorySpace.HBM) for x in (
            flux, noise_weight, pixel_owner.reshape(1, pix), pixel_cell.reshape(1, pix),
            plane_bin, bin_coeffs,
        ))
    )

    return pl.pallas_call(
        finish,
        out_shape=(out, out),
        in_specs=[vmem] * 3,
        out_specs=(vmem, vmem),
        compiler_params=pltpu.CompilerParams(vmem_limit_bytes=4 * 1024 * 1024),
        name="finish",
    )(fields, right_side, factors)


def solution(mesh):
    placed = (P("los", "tr"), P("los", "tr"), P("tr", None), P("tr"), P(), P())
    return jax.shard_map(
        local,
        mesh=mesh,
        in_specs=placed,
        out_specs=(P("los", "tr", None), P("los", "tr", None)),
        check_vma=False,
    )
```

```python
import functools

import jax
import jax.numpy as jnp
from jax import lax
from jax.experimental import pallas as pl
from jax.experimental.pallas import tpu as pltpu
from jax.sharding import PartitionSpec as P

MESH = pl.DeviceIdType.MESH
F32 = jnp.float32
BF16 = jnp.bfloat16
I32 = jnp.int32
SX = 4
CHUNK = 256
CAP = 128
MASS = 0.5
NT = (((1,), (1,)), ((), ()))


def iota(shape, dim):
    return lax.broadcasted_iota(I32, shape, dim)


def tree(parts):
    while len(parts) > 1:
        parts = [sum(parts[i + 1:i + 2], parts[i]) for i in range(0, len(parts), 2)]
    return parts[0]


def two_pieces(values):
    high = values.astype(BF16)
    return high, (values - high.astype(F32)).astype(BF16)


def roll(x, shift, axis):
    size = x.shape[axis]
    return pltpu.roll(x, shift % size if isinstance(shift, int) else shift, axis)


def kernel(
    n_tr, n_los, nzr, flux_hbm, weight_hbm, owner_hbm, cell_hbm, bin_hbm, coef_hbm,
    rb, sf, factors,
    flux_ref, weight_ref, owner_ref, cell_ref, bin_ref, coef_ref,
    hot_slot, pw, pf, rw, rf, lows, dests, acc, sw, tw, tf,
    kxs, kys, lks, base, inv, gf, zf, qf, wf, vf, pre,
    hs, hr, cs, cr, ps, p1, p2,
    load_sem, route_send, route_recv, in_send, in_recv, halo_send, halo_recv,
    out_send, out_recv, sum_send, sum_recv, fin_send, fin_recv,
):
    planes, pix = flux_ref.shape
    depth = planes * n_los
    half = depth // 2
    groups = depth // 4
    tr = lax.axis_index("tr")
    los = lax.axis_index("los")
    nyr = n_tr // nzr
    y, zc = tr // nzr, tr % nzr
    offsets = [(dy, dz) for dy in range(nyr) for dz in range(nzr)]
    offsets.sort(key=lambda o: (min(o[0], nyr - o[0]) + min(o[1], nzr - o[1]), o))
    far_steps = sorted(range(1, n_los), key=lambda d: -min(d, n_los - d))

    ring_y = [((y + d) % nyr) * nzr for d in range(nyr)]
    ring_z = [(zc + d) % nzr for d in range(nzr)]
    ring_los = [(los + d) % n_los for d in range(n_los)]

    def tr_peer(slot):
        dy, dz = offsets[slot]
        return ring_y[dy] + ring_z[dz]

    def los_peer(step):
        return ring_los[step]

    def send(src, dst, ssem, rsem, at_tr, at_los):
        return pltpu.make_async_remote_copy(
            src_ref=src, dst_ref=dst, send_sem=ssem, recv_sem=rsem,
            device_id=(at_tr, at_los), device_id_type=MESH,
        )

    barrier = pltpu.get_barrier_semaphore()
    for slot in range(n_tr - 1, 0, -1):
        pl.semaphore_signal(barrier, inc=1, device_id=(tr_peer(slot), los), device_id_type=MESH)
    for step in far_steps:
        pl.semaphore_signal(barrier, inc=1, device_id=(tr, los_peer(step)), device_id_type=MESH)

    loads = [
        pltpu.make_async_copy(src, dst, load_sem.at[n])
        for n, (src, dst) in enumerate((
            (owner_hbm, owner_ref), (weight_hbm, weight_ref), (cell_hbm, cell_ref),
            (flux_hbm, flux_ref), (bin_hbm, bin_ref), (coef_hbm, coef_ref),
        ))
    ]
    for load in loads:
        load.start()

    @pl.when(tr == 0)
    def _():
        for turn in range(2):
            hr[turn, 0] = jnp.zeros_like(hr[turn, 0])

    @pl.when(tr == n_tr - 1)
    def _():
        for turn in range(2):
            hr[turn, 1] = jnp.zeros_like(hr[turn, 1])

    @pl.when(los == 0)
    def _():
        for turn in range(2):
            cr[turn, 0] = jnp.zeros_like(cr[turn, 0])

    @pl.when(los == n_los - 1)
    def _():
        for turn in range(2):
            cr[turn, 1] = jnp.zeros_like(cr[turn, 1])

    loads[0].wait()
    owner = owner_ref[...]
    hot = jnp.where(iota((n_tr, pix), 0) == owner, 1.0, 0.0).astype(F32)
    blk = min(256, pix)
    blocks = pix // blk
    stacked = jnp.concatenate(
        [hot[:, b * blk:(b + 1) * blk] for b in range(blocks)], axis=0
    ).astype(BF16)
    before = jnp.where(iota((blk, blk), 0) < iota((blk, blk), 1), 1.0, 0.0).astype(BF16)
    prefix = jnp.dot(stacked, before, preferred_element_type=F32)
    carry = jnp.zeros((n_tr, 1), F32)
    ranks = []
    for b in range(blocks):
        part = hot[:, b * blk:(b + 1) * blk]
        ranks.append(
            jnp.sum(part * (prefix[b * n_tr:(b + 1) * n_tr] + carry), axis=0, keepdims=True)
        )
        carry = carry + jnp.sum(part, axis=1, keepdims=True)
    rank = jnp.concatenate(ranks, axis=1)
    which = owner // 2
    one = jnp.ones((16, pix), BF16)
    nothing = jnp.zeros((16, pix), BF16)
    sub16 = iota((16, pix), 0)
    lanes = (
        jnp.broadcast_to(rank.astype(I32) + CAP * (owner - 2 * which), (16, pix)) - sub16
    ).astype(F32).astype(BF16)
    for t in range(0, 2 * CAP, 16):
        hot_slot[t:t + 16, :] = jnp.where(lanes == jnp.asarray(t, BF16), one, nothing)
    pair = 16 // planes
    which16 = jnp.broadcast_to(which, (16, pix))
    mine16 = (which16 - sub16 // planes).astype(F32).astype(BF16)
    rows = n_tr // 2 * planes

    def spread_by_owner(values):
        twice = jnp.concatenate([values] * pair, axis=0)
        return [
            jnp.where(mine16 == jnp.asarray(o, BF16), twice, nothing)
            for o in range(0, n_tr // 2, pair)
        ]

    def pack(blocks):
        packed = lax.dot_general(
            jnp.concatenate(blocks, axis=0), hot_slot[...], NT, preferred_element_type=F32
        )
        count = packed.shape[0] // 2
        return packed[0:count] + packed[count:2 * count]

    def of_owner(packed, o, at, height):
        return packed[at:at + height, (o % 2) * CAP:(o % 2 + 1) * CAP]

    for load in loads[1:]:
        load.wait()
    weight = weight_ref[...]
    wa, wb = two_pieces(weight)
    ca, cb = two_pieces(cell_ref[...].astype(F32))
    here16 = (which16 - sub16).astype(F32).astype(BF16) == jnp.asarray(0, BF16)
    packed = pack([
        *spread_by_owner(wa), jnp.where(here16, jnp.broadcast_to(ca, (16, pix)), nothing),
        *spread_by_owner(wb), jnp.where(here16, jnp.broadcast_to(cb, (16, pix)), nothing),
    ])
    for o in range(n_tr):
        pw[o, 0:planes, :] = of_owner(packed, o, o // 2 * planes, planes)
        pw[o, planes:planes + 1, :] = of_owner(packed, o, rows + o // 2, 1)

    pl.semaphore_wait(barrier, n_tr - 1 + n_los - 1)

    routed = [None], [None]

    orders = (
        [*range(1, n_tr // 2), *range(n_tr - 1, n_tr // 2 - 1, -1)],
        [*range(1, n_tr // 4), *range(n_tr - 1, n_tr // 4 - 1, -1)],
    )

    def route(stage, packs, into):
        for slot in range(1, n_tr):
            peer = tr_peer(slot)
            routed[stage].append(send(
                packs.at[peer], into.at[slot],
                route_send.at[stage, slot], route_recv.at[stage, slot], peer, los,
            ))
        for slot in orders[stage]:
            routed[stage][slot].start()

    route(0, pw, rw)
    rw[0] = pw[tr]

    fa, fb = two_pieces(flux_ref[...] * weight)
    packed = pack([*spread_by_owner(fa), *spread_by_owner(fb)])
    for o in range(n_tr):
        pf[o] = of_owner(packed, o, o // 2 * planes, planes)
    route(1, pf, rf)
    rf[0] = pf[tr]

    def spread(zi, last):
        b = bin_ref[zi]
        kx = jnp.full((8, 128), coef_ref[0, b], F32)
        ky = jnp.full((8, 128), coef_ref[1, b], F32)
        link = jnp.full((8, 128), coef_ref[2, b], F32)
        link = jnp.where(zi < depth - 1, link, jnp.zeros_like(link))
        kxs[zi] = kx
        kys[zi] = ky
        lks[zi] = link
        base[zi] = MASS + 2.0 * kx + 2.0 * ky + (last + link)
        return link

    lax.fori_loop(0, depth, spread, jnp.zeros((8, 128), F32))

    width = n_los * CHUNK
    jump = min(8, n_tr)
    span = jump * CAP
    chunks = n_tr // jump
    each = SX * planes
    full = n_los * each
    upper = iota((8, span), 0) < SX
    sub_span = iota((16, span), 0)
    row16 = sub_span % SX
    ones = jnp.ones((16, span), BF16)
    none = jnp.zeros((16, span), BF16)
    upper3 = iota((planes // 2, 8, 128), 1) < SX

    def scatter(stage, g):
        arrived = (rw, rf)[stage]

        def build():
            slots = range(g * jump, (g + 1) * jump)
            if stage == 0:
                cell = jnp.concatenate([arrived[t, planes:planes + 1, :] for t in slots], axis=1)
                cell = (cell + 0.5).astype(I32)
                col = cell % width
                place = (col // CHUNK) * SX + cell // width
                low = (
                    jnp.broadcast_to(col % CHUNK, (16, span)) - sub_span
                ).astype(F32).astype(BF16)
                for t in range(0, CHUNK, 16):
                    lows[g, t:t + 16, :] = jnp.where(low == jnp.asarray(t, BF16), ones, none)
                dests[g] = (
                    jnp.broadcast_to(place, (16, span)) - row16
                ).astype(F32).astype(BF16)
            vals = jnp.concatenate([arrived[t, 0:planes, :] for t in slots], axis=1)
            ba, bb = two_pieces(jnp.concatenate([
                jnp.where(
                    upper,
                    jnp.broadcast_to(vals[p:p + 1], (8, span)),
                    jnp.broadcast_to(vals[p + 1:p + 2], (8, span)),
                )
                for p in range(0, planes, 2)
            ], axis=0))
            dest = dests[g]
            return jnp.concatenate([
                jnp.where(dest == jnp.asarray(SX * k, BF16), piece[t:t + 16], none)
                for piece in (ba, bb) for k in range(n_los) for t in range(0, each, 16)
            ], axis=0)

        def add(expanded):
            part = lax.dot_general(expanded, lows[g], NT, preferred_element_type=F32)
            part = part[0:full] + part[full:2 * full]
            if g == 0:
                acc[stage] = part
            else:
                acc[stage] = acc[stage] + part

        for slot in range(g * jump, (g + 1) * jump):
            if slot:
                routed[stage][slot].wait_recv()
        add(build())

    here = pl.ds(los * planes, planes)

    def enter(stage, out, into):
        for k in range(n_los):
            both = acc[stage, k * each:(k + 1) * each, :]
            left = both[:, 0:128].reshape(planes // 2, 8, 128)
            right = both[:, 128:256].reshape(planes // 2, 8, 128)
            even = jnp.where(upper3, left, roll(right, 4, 1))
            odd = jnp.where(upper3, roll(left, 4, 1), right)
            for p in range(planes // 2):
                out[k * planes + 2 * p] = even[p]
                out[k * planes + 2 * p + 1] = odd[p]
        copies = []
        for step in far_steps:
            peer = los_peer(step)
            copy = send(
                out.at[pl.ds(peer * planes, planes)], into.at[here],
                in_send.at[stage, step], in_recv.at[stage, step], tr, peer,
            )
            copy.start()
            copies.append(copy)
        into[here] = out[here]
        return copies

    near = max(1, chunks // 2)
    for g in (*range(near), *range(chunks - 1, near - 1, -1)):
        scatter(0, g)
    entered_w = enter(0, sw, tw)
    for g in range(chunks):
        scatter(1, g)
    entered_f = enter(1, sf, tf)

    for copy in entered_w:
        copy.wait_recv()

    stride = min(8, half)
    zero = jnp.zeros((8, 128), F32)

    def pivots(block, state):
        it, lt, ib = state
        for u in range(stride):
            zt = block * stride + u
            zb = depth - 1 - zt
            it = 1.0 / ((base[zt] + tw[zt]) - (lt * lt) * it)
            lb = lks[zb]
            ib = 1.0 / ((base[zb] + tw[zb]) - (lb * lb) * ib)
            lt = lks[zt]
            inv[zt] = it
            inv[zb] = ib
        return it, lt, ib

    it, lt, ib = lax.fori_loop(0, half // stride, pivots, (zero,) * 3)
    ratio_top, ratio_bottom = lt * it, lt * ib
    middle = 1.0 / (1.0 - ratio_top * ratio_bottom)

    def solve(source, out):
        def eliminate(block, state):
            gt, lt, gb = state
            for u in range(stride):
                zt = block * stride + u
                zb = depth - 1 - zt
                gt = (source[zt] + lt * gt) * inv[zt]
                gb = (source[zb] + lks[zb] * gb) * inv[zb]
                lt = lks[zt]
                gf[zt] = gt
                gf[zb] = gb
            return gt, lt, gb

        gt, _, gb = lax.fori_loop(0, half // stride, eliminate, (zero,) * 3)
        yt = (gt + ratio_top * gb) * middle
        yb = gb + ratio_bottom * yt
        out[half - 1] = yt
        out[half] = yb
        total = source[half - 1] * yt + source[half] * yb

        def one(zt, state):
            yt, yb, total = state
            zb = depth - 1 - zt
            yt = gf[zt] + (lks[zt] * inv[zt]) * yt
            yb = gf[zb] + (lks[zb - 1] * inv[zb]) * yb
            out[zt] = yt
            out[zb] = yb
            return yt, yb, total + (source[zt] * yt + source[zb] * yb)

        state = (yt, yb, total)
        for u in range(stride - 1):
            state = one(half - 2 - u, state)

        def some(block, state):
            for u in range(stride):
                state = one(half - 1 - (block * stride + u), state)
            return state

        return lax.fori_loop(1, half // stride, some, state)[2]

    sub = iota((8, 128), 0)
    lane = iota((8, 128), 1)
    quarter = sub % 4
    first_row, last_row = quarter == 0, quarter == 3
    in_half = sub < 4
    inner_left, inner_right = (lane == 0) & ~in_half, (lane == 127) & in_half
    outer = ((lane == 0) & in_half) | ((lane == 127) & ~in_half)

    wide = min(32, depth)
    parts = depth // wide

    def edge_copy(turn, side, kind):
        step = 1 if side == 0 else -1
        if kind < parts:
            piece = pl.ds(kind * (wide // 4), wide // 4)
            src, dst, where = hs.at[turn, side, piece], hr.at[turn, side, piece], (
                (tr + step + n_tr) % n_tr, los)
        else:
            src, dst, where = cs.at[turn], cr.at[turn, side], (tr, (los + step + n_los) % n_los)
        return send(
            src, dst, halo_send.at[turn, side, kind], halo_recv.at[turn, side, kind], *where
        )

    def edge_each(turn, kind, what):
        for side in range(2):
            copy = edge_copy(turn, side, kind)
            here_is, size = (tr, n_tr) if kind < parts else (los, n_los)
            first, last = (0, size - 1) if side == 0 else (size - 1, 0)
            if what == "start":
                pl.when(here_is != last)(copy.start)
            elif what == "sent":
                pl.when(here_is != last)(copy.wait_send)
            else:
                pl.when(here_is != first)(copy.wait_recv)


    def edge_rows(field, turn):
        for block in range(parts):
            for i in range(wide // 4):
                down = up = zero
                for j in range(4):
                    v = field[block * wide + i * 4 + j]
                    down = jnp.where(quarter == j, roll(v, j - 3, 0), down)
                    up = jnp.where(quarter == j, roll(v, j, 0), up)
                hs[turn, 0, block * (wide // 4) + i] = down
                hs[turn, 1, block * (wide // 4) + i] = up
            edge_each(turn, block, "start")

    def edge_columns(field, turn):
        def pack(block, found):
            for i in range(wide):
                zi = block * wide + i
                u = roll(field[zi], 4, 0)
                both = jnp.where(in_half, roll(u, 1, 1), u)
                found = jnp.where(lane == zi, roll(both, zi, 1), found)
            return found

        cs[turn] = lax.fori_loop(0, depth // wide, pack, zero)
        edge_each(turn, parts, "start")

    def operate_inside(field, source):
        def some(block, none):
            for i in range(wide):
                zi = block * wide + i
                v = field[zi]
                u = roll(v, 4, 0)
                up = jnp.where(first_row, 0.0, roll(v, 1, 0))
                down = jnp.where(last_row, 0.0, roll(v, -1, 0))
                before = jnp.where(inner_left, roll(u, 1, 1), roll(v, 1, 1))
                after = jnp.where(inner_right, roll(u, 127, 1), roll(v, 127, 1))
                beside = jnp.where(in_half & (lane == 0), after, before + after)
                beside = jnp.where((lane == 127) & ~in_half, before, beside)
                pre[zi] = source[zi] - (kxs[zi] * (up + down) + kys[zi] * beside)
            return none

        lax.fori_loop(0, depth // wide, some, 0)

    def operate_edges(field, turn, out):
        edge_each(turn, parts, "arrived")
        columns = jnp.where(in_half, cr[turn, 0], roll(cr[turn, 1], 127, 1))
        total = zero
        for block in range(parts):
            edge_each(turn, block, "arrived")
            for i in range(wide):
                zi = block * wide + i
                j = i % 4
                four = block * (wide // 4) + i // 4
                above, below = hr[turn, 0, four], hr[turn, 1, four]
                rows = jnp.where(
                    first_row, roll(above, -j, 0), jnp.where(last_row, roll(below, 3 - j, 0), 0.0)
                )
                beside = jnp.where(outer, roll(columns, 128 - zi, 1), 0.0)
                image = pre[zi] - (kxs[zi] * rows + kys[zi] * beside)
                out[zi] = image
                total = total + field[zi] * image
        return total

    def leave(field, which):
        copies = []
        for step in far_steps:
            peer = los_peer(step)
            copy = send(
                field.at[pl.ds(peer * planes, planes)], rb.at[which, los],
                out_send.at[which, step], out_recv.at[which, step], tr, peer,
            )
            copy.start()
            copies.append(copy)
        rb[which, los] = field[here]
        return copies

    for copy in entered_f:
        copy.wait_recv()
    dot_bz = solve(tf, zf)
    edge_rows(zf, 0)
    edge_columns(zf, 0)
    operate_inside(zf, tf)
    left_z = leave(zf, 0)
    dot_zq = operate_edges(zf, 0, qf)
    dot_qw = solve(qf, wf)
    edge_rows(wf, 1)
    edge_columns(wf, 1)
    operate_inside(wf, qf)
    left_q = leave(qf, 1)
    left_w = leave(wf, 2)
    lane1 = iota((1, 128), 1) // 32

    def part_of(dot):
        row = jnp.sum(dot, axis=0, keepdims=True)
        row = row + roll(row, 64, 1)
        return row + roll(row, 32, 1)

    mixed = jnp.where(lane1 == 0, part_of(dot_bz), part_of(dot_zq))
    mixed = jnp.where(lane1 == 2, part_of(dot_qw), mixed)
    dot_ws = operate_edges(wf, 1, vf)

    ps[0] = jnp.where(lane1 == 3, part_of(dot_ws), mixed)
    summed = []
    for slot in range(n_tr - 1, 0, -1):
        copy = send(
            ps.at[0], p1.at[slot], sum_send.at[slot], sum_recv.at[slot], tr_peer(slot), los
        )
        copy.start()
        summed.append(copy)
    left_v = leave(vf, 3)
    total = ps[0]
    for copies in (routed[0][1:], routed[1][1:], entered_w, entered_f, left_z):
        for copy in copies:
            copy.wait_send()
    for turn in range(2):
        for kind in range(parts + 1):
            edge_each(turn, kind, "sent")
    for copy in summed:
        copy.wait_recv()
    total = tree([total, *(p1[slot] for slot in range(1, n_tr))])
    ps[1] = total
    finals = []
    for step in far_steps:
        copy = send(
            ps.at[1], p2.at[step], fin_send.at[step], fin_recv.at[step], tr, los_peer(step)
        )
        copy.start()
        finals.append(copy)
    for copy in finals:
        copy.wait_recv()
    total = tree([total, *(p2[step] for step in range(1, n_los))])
    bz, zq, qw, ws = (
        jnp.broadcast_to(
            jnp.sum(jnp.where(lane1 == n, total, 0.0), axis=1, keepdims=True), (8, 128)
        )
        for n in range(4)
    )
    alpha = bz / zq
    rz = alpha * alpha * qw - bz
    beta = rz / bz
    grown = 1.0 + beta
    alpha_next = rz / (grown * grown * zq - 2.0 * grown * alpha * qw + alpha * alpha * ws)
    main = alpha + alpha_next * grown
    other = alpha * alpha_next

    for copies in (left_z, left_w, left_q, left_v):
        for copy in copies:
            copy.wait_recv()

    factors[0] = main
    factors[1] = other

    for copies in (left_q, left_w, left_v, summed, finals):
        for copy in copies:
            copy.wait_send()


def finish(rb, bf, factors, sol_ref, res_ref):
    main, other = factors[0], factors[1]
    n_los, planes = rb.shape[1:3]
    for k in range(n_los):
        for p in range(planes):
            x = main * rb[0, k, p] - other * rb[2, k, p]
            r = bf[k * planes + p] - main * rb[1, k, p] + other * rb[3, k, p]
            for part in range(2):
                at = slice(k * CHUNK + part * 128, k * CHUNK + part * 128 + 128)
                sol_ref[p, :, at] = x[part * SX:(part + 1) * SX]
                res_ref[p, :, at] = r[part * SX:(part + 1) * SX]


def local(flux, noise_weight, pixel_owner, pixel_cell, plane_bin, bin_coeffs):
    n_tr, n_los = lax.axis_size("tr"), lax.axis_size("los")
    nzr = 8 if n_tr == 32 else 2
    planes, pix = flux.shape
    depth = planes * n_los
    cols = n_los * CHUNK
    jump = min(8, n_tr)
    span = jump * CAP
    each = SX * planes
    dma = pltpu.SemaphoreType.DMA
    field = pltpu.VMEM((depth, 8, 128), F32)
    vmem = pl.BlockSpec(memory_space=pltpu.VMEM)
    hbm = pl.BlockSpec(memory_space=pltpu.MemorySpace.HBM)
    out = jax.ShapeDtypeStruct((planes, SX, cols), F32)
    fields, right_side, factors = pl.pallas_call(
        functools.partial(kernel, n_tr, n_los, nzr),
        out_shape=(
            jax.ShapeDtypeStruct((4, n_los, planes, 8, 128), F32),
            jax.ShapeDtypeStruct((depth, 8, 128), F32),
            jax.ShapeDtypeStruct((2, 8, 128), F32),
        ),
        in_specs=[hbm] * 6,
        out_specs=(vmem, vmem, vmem),
        scratch_shapes=[
            pltpu.VMEM((planes, pix), F32), pltpu.VMEM((planes, pix), F32),
            pltpu.VMEM((1, pix), I32), pltpu.VMEM((1, pix), I32),
            pltpu.SMEM(plane_bin.shape, I32), pltpu.SMEM(bin_coeffs.shape, F32),
            pltpu.VMEM((2 * CAP, pix), BF16),
            pltpu.VMEM((n_tr, planes + 1, CAP), F32),
            pltpu.VMEM((n_tr, planes, CAP), F32),
            pltpu.VMEM((n_tr, planes + 1, CAP), F32),
            pltpu.VMEM((n_tr, planes, CAP), F32),
            pltpu.VMEM((n_tr // jump, CHUNK, span), BF16),
            pltpu.VMEM((n_tr // jump, 16, span), BF16),
            pltpu.VMEM((2, n_los * each, CHUNK), F32),
            field, field, field,
            field, field, field, field, field, field, field, field, field, field, field,
            pltpu.VMEM((2, 2, depth // 4, 8, 128), F32),
            pltpu.VMEM((2, 2, depth // 4, 8, 128), F32),
            pltpu.VMEM((2, 8, 128), F32),
            pltpu.VMEM((2, 2, 8, 128), F32),
            pltpu.VMEM((2, 1, 128), F32),
            pltpu.VMEM((n_tr, 1, 128), F32),
            pltpu.VMEM((n_los, 1, 128), F32),
            dma((6,)), dma((2, n_tr)), dma((2, n_tr)), dma((2, n_los)), dma((2, n_los)),
            dma((2, 2, 3)), dma((2, 2, 3)), dma((4, n_los)), dma((4, n_los)),
            dma((n_tr,)), dma((n_tr,)), dma((n_los,)), dma((n_los,)),
        ],
        compiler_params=pltpu.CompilerParams(
            collective_id=0, has_side_effects=True, vmem_limit_bytes=50 * 1024 * 1024
        ),
        name="wiener",
    )(
        *(pltpu.with_memory_space_constraint(x, pltpu.MemorySpace.HBM) for x in (
            flux, noise_weight, pixel_owner.reshape(1, pix), pixel_cell.reshape(1, pix),
            plane_bin, bin_coeffs,
        ))
    )

    return pl.pallas_call(
        finish,
        out_shape=(out, out),
        in_specs=[vmem] * 3,
        out_specs=(vmem, vmem),
        compiler_params=pltpu.CompilerParams(vmem_limit_bytes=4 * 1024 * 1024),
        name="finish",
    )(fields, right_side, factors)


def solution(mesh):
    placed = (P("los", "tr"), P("los", "tr"), P("tr", None), P("tr"), P(), P())
    return jax.shard_map(
        local,
        mesh=mesh,
        in_specs=placed,
        out_specs=(P("los", "tr", None), P("los", "tr", None)),
        check_vma=False,
    )
```
